256 devices in a mesh: depth: 8 (over x, core), rows: 32 (over z, y).
Axes of the slice: x: 4, y: 4, z: 8, core: 2. Of those that a mesh axis runs over, the one named last changes fastest.
Arguments:
- source_top: bfloat16 [2, 2, 512, 512], P(None, None, 'rows'), may hold values from -8 to 8
- adjoint_bottom: bfloat16 [2, 2, 512, 512], P(None, None, 'rows'), may hold values from -8 to 8
- slowness: float32 [8, 512, 512], P('depth', 'rows'), may hold values from 0.7 to 1.3
- correction: float32 [8, 512, 512], P('depth', 'rows'), may hold values from -0.16 to 0.16
- slowness_ref: float32 [8], P('depth'), may hold values from 0.9 to 1.1
- omega: float32 [2], replicated, may hold values from 0.8 to 1.6
Outputs:
- gradient: float32 [8, 512, 512], P('depth', 'rows')
The draws below stay inside these ranges and needn't reach their ends.
All inputs are finite; a program needn't handle non-finite values.
Results may differ from the reference program's by a relative error of at most 0.025.
Values may be sent and summed in bfloat16 or wider, within the bound.
A program may use at most 64 MiB of HBM per device.

```python
import math
import jax
import jax.numpy as jnp
from jax import lax

NX = 512
NY = 512
NF = 2
NZ = 8


def steps_of(rng, extent, split, low, largest):
    def one(dim, parts):
        draws = jax.random.uniform(jax.random.fold_in(jax.random.fold_in(rng, 6), dim), (parts,), jnp.float32, low / len(split), largest / len(split))
        return jnp.repeat(jnp.exp(draws), extent[dim] // parts).reshape((-1,) + (1,) * (len(extent) - dim - 1))

    level = one(*split[0])
    for cut in split[1:]:
        level = level * one(*cut)
    return level


def normal_values(rng, shape, deviation, reach, cuts=(), held_as=jnp.bfloat16):
    drawn = deviation * jax.random.normal(rng, shape, jnp.float32)
    if cuts:
        drawn = drawn * steps_of(rng, shape, cuts, -0.22, 0.18)
    return jnp.clip(drawn, -reach, reach).astype(held_as)


def setup_inputs(seed: int = 0) -> dict:
    arg_keys = jax.random.split(jax.random.key(seed), 7)
    return {
        "source_top": normal_values(arg_keys[0], (NF, 2, NX, NY), 2.0, 8.0, ((2, 32),)),
        "adjoint_bottom": normal_values(arg_keys[1], (NF, 2, NX, NY), 2.0, 8.0, ((2, 32),)),
        "slowness": jnp.clip(0.7 + 0.59999996 * jax.random.uniform(arg_keys[2], (NZ, NX, NY), jnp.float32) ** steps_of(arg_keys[2], (NZ, NX, NY), ((0, 8), (1, 32)), -0.2, 0.2), 0.7, 1.3),
        "correction": jnp.clip(jax.random.uniform(arg_keys[3], (NZ, NX, NY), jnp.float32, -0.16, 0.16) * steps_of(arg_keys[3], (NZ, NX, NY), ((0, 8), (1, 32)), -0.4, 0.0), -0.16, 0.16),
        "slowness_ref": jnp.clip(0.9 + 0.20000005 * jax.random.uniform(arg_keys[4], (NZ,), jnp.float32) ** steps_of(arg_keys[4], (NZ,), ((0, 8),), -0.2, 0.2), 0.9, 1.1),
        "omega": jnp.clip(jnp.exp(jax.random.uniform(arg_keys[5], (NF,), jnp.float32, math.log(0.8), math.log(1.6))), 0.8, 1.6),
    }


depth_step = 1.0

def rounded(values):
    return lax.optimization_barrier(values.astype(jnp.bfloat16)).astype(jnp.float32)

def rounded_complex(values):
    return rounded(jnp.real(values)) + 1j * rounded(jnp.imag(values))

def wavenumbers(length):
    positions = jnp.arange(length, dtype=jnp.int32)
    signed = jnp.where(positions >= length // 2, positions - length, positions)
    return signed.astype(jnp.float32) * (2.0 * math.pi / length)

def phase_for(omega_value, reference_slow):
    wave_x = wavenumbers(NX)[:, None]
    wave_y = wavenumbers(NY)[None, :]
    squared = (omega_value * reference_slow) ** 2 - wave_x ** 2 - wave_y ** 2
    damping = jnp.exp(-jnp.sqrt(jnp.maximum(-squared, 0.0)) * depth_step)
    angles = jnp.sqrt(jnp.maximum(squared, 0.0)) * depth_step
    return damping * jnp.cos(angles) + 1j * (damping * jnp.sin(angles))

def transform(values):
    half_way = rounded_complex(jnp.fft.fft(values, axis=1, norm='ortho'))
    return jnp.fft.fft(half_way, axis=0, norm='ortho')

def inverse(values):
    half_way = rounded_complex(jnp.fft.ifft(values, axis=0, norm='ortho'))
    return jnp.fft.ifft(half_way, axis=1, norm='ortho')

def laplace(values):
    return jnp.roll(values, 1, 0) + jnp.roll(values, -1, 0) + jnp.roll(values, 1, 1) + jnp.roll(values, -1, 1) - 4.0 * values

def reference(source_top, adjoint_bottom, slowness, correction, slowness_ref, omega):
    gradient = [jnp.zeros((NX, NY), jnp.float32) for depth_level in range(NZ)]
    for frequency in range(NF):
        omega_value = omega[frequency]
        phases = [phase_for(omega_value, slowness_ref[depth_level]) for depth_level in range(NZ)]
        lenses = []
        for depth_level in range(NZ):
            angles = omega_value * (slowness[depth_level] - slowness_ref[depth_level]) * depth_step
            lenses.append(jnp.cos(angles) + 1j * jnp.sin(angles))
        plane = source_top[frequency, 0].astype(jnp.float32) + 1j * source_top[frequency, 1].astype(jnp.float32)
        planes_below = []
        for depth_level in range(NZ):
            lensed = lenses[depth_level] * inverse(phases[depth_level] * transform(plane))
            scaled = rounded_complex(correction[depth_level] * lensed)
            plane = rounded_complex(lensed + 1j * laplace(scaled))
            planes_below.append(plane)
        adjoint = adjoint_bottom[frequency, 0].astype(jnp.float32) + 1j * adjoint_bottom[frequency, 1].astype(jnp.float32)
        for depth_level in reversed(range(NZ)):
            below_plane = planes_below[depth_level]
            product = jnp.real(below_plane) * jnp.imag(adjoint) - jnp.imag(below_plane) * jnp.real(adjoint)
            gradient[depth_level] = gradient[depth_level] + omega_value * product
            pulled = jnp.conj(lenses[depth_level]) * (adjoint - 1j * correction[depth_level] * laplace(adjoint))
            adjoint = rounded_complex(inverse(jnp.conj(phases[depth_level]) * transform(pulled)))
    return jnp.stack(gradient).astype(jnp.float32)
```

```python
import math

import jax
import jax.numpy as jnp
from jax import lax
from jax.experimental import pallas as pl
from jax.experimental.pallas import tpu as pltpu
from jax.sharding import PartitionSpec as P

MESH = pl.DeviceIdType.MESH
f32, bf16 = jnp.float32, jnp.bfloat16
HALF = 256
ROWS = 16
NROW = 32
NZ = 8
REF_ROW = 5
CHAINS = ((1, 0), (2, 9), (4, 18), (6, 27))


def chain_depth(c):
    return jnp.where(c == 0, 1, 2 * c)


def chain_row(c):
    return 9 * c


def is_chain_device(d, r):
    hit = jnp.logical_and(d == CHAINS[0][0], r == CHAINS[0][1])
    for cd, cr in CHAINS[1:]:
        hit = jnp.logical_or(hit, jnp.logical_and(d == cd, r == cr))
    return hit


def dot(a, b, precision=None):
    return jnp.dot(a, b, preferred_element_type=f32, precision=precision)


def iota2(shape, dim):
    return lax.broadcasted_iota(jnp.int32, shape, dim)


def exchange(size, flipped=True):
    row, col = iota2((size, size), 0), iota2((size, size), 1)
    target = jnp.where(flipped, size - 1 - row, row)
    return jnp.where(col == target, 1.0, 0.0).astype(f32)


def series(t, coefs):
    total = jnp.full_like(t, coefs[-1])
    for coef in coefs[-2::-1]:
        total = total * t + coef
    return total


COS_LENS = [(-1.0) ** k / math.factorial(2 * k) for k in range(5)]
SIN_LENS = [(-1.0) ** k / math.factorial(2 * k + 1) for k in range(5)]
COS_PHASE = [(-1.0) ** k / math.factorial(2 * k) for k in range(9)]
SIN_PHASE = [(-1.0) ** k / math.factorial(2 * k + 1) for k in range(8)]


def row_slot(r):
    side = r // 16
    block = jnp.where(side == 1, 31 - r, r)
    return side, pl.ds(pl.multiple_of(block * ROWS, ROWS), ROWS)


def kernel(
    slow_ref, corr_ref, src_ref, adj_ref, ref_ref, omega_ref, out_ref,
    prep, prep_plane, prep_slow,
    coef, plane, refs, arrived,
    phase, base, base_t, table, table_t, ridge,
    shipped, xb, gb, eb, wb,
    prep_sem, prep_plane_sem, prep_slow_sem,
    coef_sem, plane_sem, refs_sem, arrived_sem, ship_sem, ask_sem,
):
    d = lax.axis_index("depth")
    r = lax.axis_index("rows")
    side = r // 16
    barrier = pltpu.get_barrier_semaphore()
    chain_here = is_chain_device(d, r)
    me_c = jnp.where(d == 1, 0, d // 2)

    @pl.when(chain_here)
    def _():
        first = jnp.where(me_c < 2, 0, NZ - 1)

        @pl.loop(0, NROW)
        def _(i):
            pl.semaphore_signal(barrier, inc=1, device_id=(first, i), device_id_type=MESH)

        @pl.loop(0, NZ)
        def _(i):
            @pl.when(i != first)
            def _():
                pl.semaphore_signal(barrier, inc=1, device_id=(i, REF_ROW), device_id_type=MESH)

    for c, (cd, cr) in enumerate(CHAINS):
        @pl.when(jnp.logical_or(d != cd, r != cr))
        def _():
            pl.semaphore_signal(barrier, inc=1, device_id=(cd, cr), device_id_type=MESH)

    turn = exchange(ROWS, side == 1)
    flip = exchange(HALF).astype(bf16)
    turn_b = turn.astype(bf16)

    def halves(values):
        turned = dot(turn_b, values).astype(bf16)
        return turned[:, :HALF], dot(turned[:, HALF:], flip).astype(bf16)

    slow_value = ref_ref[0]
    for k, values in enumerate((slow_ref[0] - slow_value, corr_ref[0])):
        left, right = halves(values.astype(bf16))
        prep[k, 0] = left
        prep[k, 1] = right
    prep_slow[...] = jnp.full((8, 128), slow_value, f32)

    def send_prep(c):
        slot_side, slot_rows = row_slot(r)
        return pltpu.make_async_remote_copy(
            prep, coef.at[d, :, :, slot_side, slot_rows, :], prep_sem.at[c], coef_sem.at[d],
            device_id=(chain_depth(c), chain_row(c)), device_id_type=MESH,
        )

    def send_plane(c):
        slot_side, slot_rows = row_slot(r)
        return pltpu.make_async_remote_copy(
            prep_plane.at[c % 2], plane.at[:, :, slot_side, slot_rows, :], prep_plane_sem.at[c % 2], plane_sem,
            device_id=(chain_depth(c), chain_row(c)), device_id_type=MESH,
        )

    def send_slow(c):
        return pltpu.make_async_remote_copy(
            prep_slow, refs.at[d], prep_slow_sem.at[c], refs_sem,
            device_id=(chain_depth(c), chain_row(c)), device_id_type=MESH,
        )

    at_end = jnp.logical_or(d == 0, d == NZ - 1)
    first_chain = jnp.where(d == 0, 0, 2)

    def asked_by(c):
        return jnp.logical_and(d != 0, jnp.logical_or(d != NZ - 1, c < 2))

    @pl.when(d == 0)
    def _():
        for w in range(2):
            for k in range(2):
                left, right = halves(src_ref[w, k])
                prep_plane[w, k, 0] = left
                prep_plane[w, k, 1] = right

    @pl.when(d == NZ - 1)
    def _():
        for w in range(2):
            for k in range(2):
                left, right = halves(adj_ref[w, k])
                prep_plane[w, k, 0] = left
                prep_plane[w, k, 1] = right

    @pl.when(r == REF_ROW)
    def _():
        pl.semaphore_wait(barrier, 4)

        @pl.loop(0, 4)
        def _(c):
            send_slow(c).start()

    @pl.when(jnp.logical_and(at_end, r != REF_ROW))
    def _():
        pl.semaphore_wait(barrier, 2)

    @pl.when(at_end)
    def _():
        for w in range(2):
            send_plane(first_chain + w).start()
        for w in range(2):
            send_prep(first_chain + w).start()

    @pl.when(jnp.logical_not(chain_here))
    def _():
        start = jnp.where(d >= NZ // 2, 2, 0)

        @pl.loop(0, 4)
        def _(i):
            c = lax.rem(i + start, 4)

            @pl.when(asked_by(c))
            def _():
                pl.semaphore_wait(ask_sem.at[c], 1)
                send_prep(c).start()

    def run_chain(source):
        w = me_c % 2
        omega = omega_ref[w]

        def depth_of(step):
            return step if source else NZ - 1 - step

        def ask(depth):
            @pl.loop(0, NROW)
            def _(i):
                @pl.when(jnp.logical_not(is_chain_device(depth, i)))
                def _():
                    pl.semaphore_signal(ask_sem.at[me_c], inc=1, device_id=(depth, i), device_id_type=MESH)

        for p in range(2):
            for dest, dims in ((base, (0, 1)), (base_t, (1, 0))):
                n = iota2((HALF, HALF), dims[0])
                k = iota2((HALF, HALF), dims[1])
                if p == 1:
                    k = jnp.where(k == 0, HALF, k)
                angle = ((2 * n + 1) * k % (4 * HALF)).astype(f32) * (2.0 * math.pi / (4 * HALF))
                dest[p] = (jnp.cos(angle) if p == 0 else jnp.sin(angle)) * 0.0625
            row, col = iota2((HALF, HALF), 0), iota2((HALF, HALF), 1)
            near = jnp.where(jnp.abs(row - col) == 1, 1.0, jnp.where(row == col, -2.0, 0.0))
            corner = jnp.logical_and(row == col, jnp.logical_or(row == 0, row == HALF - 1))
            ridge[p] = jnp.where(corner, -1.0 if p == 0 else -3.0, near).astype(bf16)

        pl.semaphore_wait(barrier, 255)
        for c in range(4):
            @pl.when(c != me_c)
            def _():
                send_prep(c).start()
        slot_side, slot_rows = row_slot(r)
        own = pltpu.make_async_copy(prep, coef.at[d, :, :, slot_side, slot_rows, :], coef_sem.at[d])
        own.start()
        ask(depth_of(1))

        pltpu.make_async_copy(refs, refs, refs_sem).wait()

        unit = 2.0 * math.pi / (2 * HALF)

        def scale_power(depth):
            return (14 * depth) % 16, (14 * depth + 7) % 16

        @pl.loop(0, NZ)
        def _(depth):
            speed = refs[depth, 0:1, 0:1] * omega
            speed2 = speed * speed
            forward_power, inverse_power = scale_power(depth)
            power = (forward_power + inverse_power).astype(f32)
            gain = jnp.exp2(jnp.full((1, 1), 1.0, f32) * power * (-0.125))

            def phase_tile(row, col, row_odd, col_odd):
                gains = gain * jnp.where(row == 0, 0.5, 1.0) * jnp.where(col == 0, 0.5, 1.0)
                row = jnp.where(row == 0, HALF, row) if row_odd else row
                col = jnp.where(col == 0, HALF, col) if col_odd else col
                wave_x, wave_y = row.astype(f32) * unit, col.astype(f32) * unit
                squared = speed2 - wave_x * wave_x - wave_y * wave_y
                damping = jnp.exp(-jnp.sqrt(jnp.maximum(-squared, 0.0))) * gains
                inside = jnp.maximum(squared, 0.0)
                angle = jnp.sqrt(inside)
                return damping * series(inside, COS_PHASE), damping * (series(inside, SIN_PHASE) * angle)

            @pl.loop(0, HALF // 8)
            def _(i):
                rows = pl.ds(pl.multiple_of(i * 8, 8), 8)
                row = iota2((8, HALF), 0) + i * 8
                col = iota2((8, HALF), 1)
                even = phase_tile(row, col, False, False)
                odd = phase_tile(row[:, :128], col[:, :128], False, True)
                for k in range(2):
                    for p in range(2):
                        phase[depth, 0, p, k, rows, :] = even[k]
                        phase[depth, 1, p, k, rows, 0:128] = odd[k]
                        phase[depth, 1, p, k, rows, 128:256] = even[k][:, 128:]

            row, col = iota2((8, HALF), 0), iota2((8, HALF), 1)
            for q in range(2):
                tile = phase_tile(row, col, True, q == 1)
                for k in range(2):
                    phase[depth, q, 1, k, 0:8, :] = tile[k]

        def make_tables(depth):
            forward_power, inverse_power = scale_power(depth)
            for way, power in enumerate((forward_power, inverse_power)):
                scale = jnp.exp2(jnp.full((1, 1), 1.0, f32) * power.astype(f32) * 0.0625)
                for p in range(2):
                    table[way, p] = (base[p] * scale).astype(bf16)
                    table_t[way, p] = (base_t[p] * scale).astype(bf16)

        def propagate(depth):
            for q in range(2):
                for p in range(2):
                    half = dot(xb[q, p].reshape(2 * HALF, HALF), table[0, q]).astype(bf16)
                    real = dot(table_t[0, p], half[:HALF])
                    imag = dot(table_t[0, p], half[HALF:])
                    cos = phase[depth, q, p, 0]
                    sin = phase[depth, q, p, 1]
                    if source:
                        turned = (real * cos - imag * sin, real * sin + imag * cos)
                    else:
                        turned = (real * cos + imag * sin, imag * cos - real * sin)
                    back = [dot(table[1, p], part.astype(bf16)).astype(bf16) for part in turned]
                    for k in range(2):
                        eb[q, p, k] = dot(back[k], table_t[1, q])

        def laplace(blocks, q, p, k):
            values = blocks[q, p, k]
            return dot(values, ridge[q]) + dot(ridge[p], values)

        def unfold(parts):
            mixed = [[parts[q][0] + parts[q][1], parts[q][0] - parts[q][1]] for q in range(2)]
            return [[mixed[0][a] + mixed[1][a] for a in range(2)], [mixed[0][a] - mixed[1][a] for a in range(2)]]

        def tiles(body):
            @pl.loop(0, HALF // ROWS)
            def _(i):
                rows = pl.ds(pl.multiple_of(i * ROWS, ROWS), ROWS)
                for j in range(2):
                    body(rows, pl.ds(j * 128, 128))

        def lens_of(depth, b, a, rows, cols):
            angle = coef[depth, 0, b, a, rows, cols].astype(f32) * omega
            square = angle * angle
            return series(square, COS_LENS), series(square, SIN_LENS) * angle

        def ship(step, depth):
            @pl.loop(0, NROW)
            def _(i):
                to_side, to_rows = row_slot(i)
                block = shipped.at[step, :, :, to_side, to_rows, :]
                here = jnp.logical_and(depth == d, i == r)

                @pl.when(here)
                def _():
                    pltpu.make_async_copy(block, arrived.at[me_c], ship_sem.at[step]).start()

                @pl.when(jnp.logical_not(here))
                def _():
                    pltpu.make_async_remote_copy(
                        block, arrived.at[me_c], ship_sem.at[step], arrived_sem.at[me_c],
                        device_id=(depth, i), device_id_type=MESH,
                    ).start()

        def ask_ahead(step):
            @pl.when(step + 2 < steps)
            def _():
                ask(depth_of(step + 2))

        def wait_coef(depth):
            pltpu.make_async_copy(coef.at[depth], coef.at[depth], coef_sem.at[depth]).wait()

        steps = NZ if source else NZ - 1
        pltpu.make_async_copy(plane, plane, plane_sem).wait()

        def first_fold(rows, cols):
            for k in range(2):
                folded = unfold([[plane[k, b, a, rows, cols].astype(f32) for a in range(2)] for b in range(2)])
                for q in range(2):
                    for p in range(2):
                        if source:
                            xb[q, p, k, rows, cols] = folded[q][p].astype(bf16)
                        else:
                            eb[q, p, k, rows, cols] = folded[q][p] * 0.25
                            gb[q, p, k, rows, cols] = (folded[q][p] * 0.25).astype(bf16)

        tiles(first_fold)

        if source:
            @pl.loop(0, steps)
            def _(step):
                depth = depth_of(step)
                make_tables(depth)
                ask_ahead(step)
                propagate(depth)
                wait_coef(depth)

                def spatial(rows, cols):
                    real = unfold([[eb[q, p, 0, rows, cols] for p in range(2)] for q in range(2)])
                    imag = unfold([[eb[q, p, 1, rows, cols] for p in range(2)] for q in range(2)])
                    lensed = [[[None, None], [None, None]] for _ in range(2)]
                    scaled = [[[None, None], [None, None]] for _ in range(2)]
                    for b in range(2):
                        for a in range(2):
                            cos, sin = lens_of(depth, b, a, rows, cols)
                            factor = coef[depth, 1, b, a, rows, cols].astype(f32)
                            lensed[0][b][a] = real[b][a] * cos - imag[b][a] * sin
                            lensed[1][b][a] = real[b][a] * sin + imag[b][a] * cos
                            for k in range(2):
                                scaled[k][b][a] = lensed[k][b][a] * factor
                    for k in range(2):
                        wave, bend = unfold(lensed[k]), unfold(scaled[k])
                        for q in range(2):
                            for p in range(2):
                                wb[q, p, k, rows, cols] = wave[q][p]
                                gb[q, p, k, rows, cols] = bend[q][p].astype(bf16)

                tiles(spatial)
                for q in range(2):
                    new = []
                    for p in range(2):
                        real = wb[q, p, 0] - laplace(gb, q, p, 1)
                        imag = wb[q, p, 1] + laplace(gb, q, p, 0)
                        xb[q, p, 0] = real.astype(bf16)
                        xb[q, p, 1] = imag.astype(bf16)
                        new.append((real * 0.25, imag * 0.25))
                    for k in range(2):
                        shipped[step, q, k, 0] = (new[0][k] + new[1][k]).astype(bf16)
                        shipped[step, q, k, 1] = (new[0][k] - new[1][k]).astype(bf16)
                ship(step, depth)
        else:
            @pl.loop(0, steps)
            def _(step):
                depth = depth_of(step)
                make_tables(depth)
                ask_ahead(step)
                for q in range(2):
                    for p in range(2):
                        for k in range(2):
                            wb[q, p, k] = laplace(gb, q, p, k)
                wait_coef(depth)

                def spatial(rows, cols):
                    value = [unfold([[eb[q, p, k, rows, cols] for p in range(2)] for q in range(2)]) for k in range(2)]
                    bend = [unfold([[wb[q, p, k, rows, cols] for p in range(2)] for q in range(2)]) for k in range(2)]
                    pulled = [[[None, None], [None, None]] for _ in range(2)]
                    for b in range(2):
                        for a in range(2):
                            cos, sin = lens_of(depth, b, a, rows, cols)
                            factor = coef[depth, 1, b, a, rows, cols].astype(f32)
                            real = value[0][b][a] + factor * bend[1][b][a]
                            imag = value[1][b][a] - factor * bend[0][b][a]
                            pulled[0][b][a] = real * cos + imag * sin
                            pulled[1][b][a] = imag * cos - real * sin
                    for k in range(2):
                        folded = unfold(pulled[k])
                        for q in range(2):
                            for p in range(2):
                                xb[q, p, k, rows, cols] = folded[q][p].astype(bf16)

                tiles(spatial)
                propagate(depth)

                def finish(rows, cols):
                    for q in range(2):
                        for k in range(2):
                            even, odd = eb[q, 0, k, rows, cols], eb[q, 1, k, rows, cols]
                            gb[q, 0, k, rows, cols] = even.astype(bf16)
                            gb[q, 1, k, rows, cols] = odd.astype(bf16)
                            shipped[step, q, k, 0, rows, cols] = (even + odd).astype(bf16)
                            shipped[step, q, k, 1, rows, cols] = (even - odd).astype(bf16)

                tiles(finish)
                ship(step, depth - 1)

        @pl.loop(0, steps)
        def _(step):
            pltpu.make_async_copy(shipped.at[step], shipped.at[step], ship_sem.at[step]).wait()

    @pl.when(jnp.logical_and(chain_here, me_c < 2))
    def _():
        run_chain(True)

    @pl.when(jnp.logical_and(chain_here, me_c >= 2))
    def _():
        run_chain(False)

    def arrival(c):
        @pl.when(jnp.logical_not(jnp.logical_and(chain_here, me_c == c)))
        def _():
            pltpu.make_async_copy(arrived.at[c], arrived.at[c], arrived_sem.at[c]).wait()

    for c in range(2):
        arrival(c)

    @pl.when(d != NZ - 1)
    def _():
        for c in range(2, 4):
            arrival(c)

    last = d == NZ - 1
    total = [None, None]
    for w in range(2):
        below = [[arrived[w, q, k].astype(f32) for k in range(2)] for q in range(2)]
        above = [[arrived[2 + w, q, k].astype(f32) for k in range(2)] for q in range(2)]
        for b in range(2):
            sign = 1.0 if b == 0 else -1.0
            down = [below[0][k] + sign * below[1][k] for k in range(2)]
            up = [
                jnp.where(last, prep_plane[w, k, b].astype(f32), above[0][k] + sign * above[1][k])
                for k in range(2)
            ]
            term = omega_ref[w] * (down[0] * up[1] - down[1] * up[0])
            total[b] = term if total[b] is None else total[b] + term
    exact = lax.Precision.HIGHEST
    total = [dot(turn, part, exact) for part in total]
    out_ref[:, :HALF] = total[0]
    out_ref[:, HALF:] = dot(total[1], exchange(HALF), exact)

    @pl.loop(0, 4)
    def _(c):
        @pl.when(jnp.logical_and(jnp.logical_not(jnp.logical_and(chain_here, me_c == c)), jnp.logical_or(d != 0, c < 2)))
        def _():
            send_prep(c).wait_send()

        @pl.when(r == REF_ROW)
        def _():
            send_slow(c).wait_send()

    @pl.when(at_end)
    def _():
        for w in range(2):
            send_plane(first_chain + w).wait_send()


def per_device(source_top, adjoint_bottom, slowness, correction, slowness_ref, omega):
    vmem = pl.BlockSpec(memory_space=pltpu.VMEM)
    smem = pl.BlockSpec(memory_space=pltpu.SMEM)
    dma, plain = pltpu.SemaphoreType.DMA, pltpu.SemaphoreType.REGULAR
    block = (HALF, HALF)
    gradient = pl.pallas_call(
        kernel,
        out_shape=jax.ShapeDtypeStruct((ROWS, 2 * HALF), f32),
        in_specs=[vmem, vmem, vmem, vmem, smem, smem],
        out_specs=vmem,
        scratch_shapes=[
            pltpu.VMEM((2, 2, ROWS, HALF), bf16),
            pltpu.VMEM((2, 2, 2, ROWS, HALF), bf16),
            pltpu.VMEM((8, 128), f32),
            pltpu.VMEM((NZ, 2, 2, 2) + block, bf16),
            pltpu.VMEM((2, 2, 2) + block, bf16),
            pltpu.VMEM((NZ, 8, 128), f32),
            pltpu.VMEM((4, 2, 2, ROWS, HALF), bf16),
            pltpu.VMEM((NZ, 2, 2, 2) + block, f32),
            pltpu.VMEM((2,) + block, f32),
            pltpu.VMEM((2,) + block, f32),
            pltpu.VMEM((2, 2) + block, bf16),
            pltpu.VMEM((2, 2) + block, bf16),
            pltpu.VMEM((2,) + block, bf16),
            pltpu.VMEM((NZ, 2, 2, 2) + block, bf16),
            pltpu.VMEM((2, 2, 2) + block, bf16),
            pltpu.VMEM((2, 2, 2) + block, bf16),
            pltpu.VMEM((2, 2, 2) + block, f32),
            pltpu.VMEM((2, 2, 2) + block, f32),
            dma((4,)),
            dma((2,)),
            dma((4,)),
            dma((NZ,)),
            dma(()),
            dma(()),
            dma((4,)),
            dma((NZ,)),
            plain((4,)),
        ],
        compiler_params=pltpu.CompilerParams(
            collective_id=0, has_side_effects=True, vmem_limit_bytes=60 * 1024 * 1024
        ),
        name="imaging",
    )(slowness, correction, source_top, adjoint_bottom, slowness_ref, omega)
    return gradient[None]


def solution(mesh):
    in_specs = (
        P(None, None, "rows", None),
        P(None, None, "rows", None),
        P("depth", "rows", None),
        P("depth", "rows", None),
        P("depth"),
        P(),
    )
    return jax.shard_map(
        per_device, mesh=mesh, in_specs=in_specs, out_specs=P("depth", "rows", None), check_vma=False
    )
```

```python
import math

import jax
import jax.numpy as jnp
from jax import lax
from jax.experimental import pallas as pl
from jax.experimental.pallas import tpu as pltpu
from jax.sharding import PartitionSpec as P

MESH = pl.DeviceIdType.MESH
f32, bf16 = jnp.float32, jnp.bfloat16
HALF = 256
ROWS = 16
NROW = 32
NZ = 8
REF_ROW = 5


def chain_depth(c):
    return 2 + 2 * (c % 2)


def chain_row(c):
    return 9 * c


def on_chain_chip(d, r):
    return jnp.logical_and(r % 9 == 0, d // 2 == 1 + (r // 9) % 2)


def on_edge(d, r):
    c = r // 8
    even = jnp.logical_and((r // 4) % 2 == 0, (r + c) % 2 == 1)
    return jnp.logical_and(even, d == 3 + 2 * (c % 2))


def unasked(d, r):
    return jnp.logical_or(on_chain_chip(d, r), on_edge(d, r))


def dot(a, b, precision=None):
    return jnp.dot(a, b, preferred_element_type=f32, precision=precision)


def iota2(shape, dim):
    return lax.broadcasted_iota(jnp.int32, shape, dim)


def exchange(size, flipped=True):
    row, col = iota2((size, size), 0), iota2((size, size), 1)
    target = jnp.where(flipped, size - 1 - row, row)
    return jnp.where(col == target, 1.0, 0.0).astype(f32)


def series(t, coefs):
    total = jnp.full_like(t, coefs[-1])
    for coef in coefs[-2::-1]:
        total = total * t + coef
    return total


COS_LENS = [(-1.0) ** k / math.factorial(2 * k) for k in range(5)]
SIN_LENS = [(-1.0) ** k / math.factorial(2 * k + 1) for k in range(5)]
COS_PHASE = [(-1.0) ** k / math.factorial(2 * k) for k in range(9)]
SIN_PHASE = [(-1.0) ** k / math.factorial(2 * k + 1) for k in range(8)]


def row_slot(r):
    side = r // 16
    block = jnp.where(side == 1, 31 - r, r)
    return side, pl.ds(pl.multiple_of(block * ROWS, ROWS), ROWS)


def kernel(
    slow_ref, corr_ref, src_ref, adj_ref, ref_ref, omega_ref, out_ref,
    prep, prep_plane, prep_slow,
    coef, plane, refs, arrived,
    phase, base, base_t, table, table_t, ridge,
    shipped, xb, gb, eb, wb,
    prep_sem, prep_plane_sem, prep_slow_sem,
    coef_sem, plane_sem, refs_sem, arrived_sem, ship_sem, ask_sem, landed_sem, spread_sem, phase_sem, phase_out_sem,
    edge_sem, ready_sem, relayed, relayed_plane, relay_sem, relay_plane_sem, onward_sem, onward_plane_sem,
):
    d = lax.axis_index("depth")
    r = lax.axis_index("rows")
    side = r // 16
    barrier = pltpu.get_barrier_semaphore()
    z, y = r // 4, r % 4
    me_c = z // 2
    chip_here = on_chain_chip(d, r)
    chain_here = jnp.logical_and(chip_here, d % 2 == 0)
    helper_here = jnp.logical_and(chip_here, d % 2 == 1)
    edge_here = on_edge(d, r)
    relay_here = d == 3 + 2 * (y % 2)
    at_end = jnp.logical_or(d == 0, d == NZ - 1)
    first_chain = jnp.where(d == 0, 0, 2)
    far_c = (y + 2) % 4

    def greet(depth, row):
        pl.semaphore_signal(barrier, inc=1, device_id=(depth, row), device_id_type=MESH)

    @pl.when(chain_here)
    def _():
        first = jnp.where(me_c < 2, 0, NZ - 1)

        @pl.loop(0, NROW)
        def _(i):
            greet(first, i)

        @pl.loop(0, 8)
        def _(i):
            @pl.when(i != z)
            def _():
                greet(d + 1, 4 * i + y)

        for c in range(4):
            @pl.when(c != me_c)
            def _():
                greet(chain_depth(c), chain_row(c))
            for other in (1, 3):
                greet(chain_depth(c) + 1, 8 * c + (c + other) % 4)

    @pl.when(relay_here)
    def _():
        @pl.loop(0, NZ)
        def _(i):
            greet(i, 4 * z + far_c)

    @pl.when(helper_here)
    def _():
        greet(d - 1, r)

        @pl.loop(0, NZ)
        def _(i):
            greet(i, REF_ROW)

    @pl.when(edge_here)
    def _():
        greet(d - 1, 9 * me_c)

    for c in range(4):
        @pl.when(jnp.logical_or(d != chain_depth(c) + 1, r != chain_row(c)))
        def _():
            greet(chain_depth(c) + 1, chain_row(c))

    turn = exchange(ROWS, side == 1)
    flip = exchange(HALF).astype(bf16)
    turn_b = turn.astype(bf16)

    def halves(values):
        turned = dot(turn_b, values).astype(bf16)
        return turned[:, :HALF], dot(turned[:, HALF:], flip).astype(bf16)

    slow_value = ref_ref[0]
    for k, values in enumerate((slow_ref[0] - slow_value, corr_ref[0])):
        left, right = halves(values.astype(bf16))
        prep[k, 0] = left
        prep[k, 1] = right
    prep_slow[...] = jnp.full((8, 128), slow_value, f32)

    def send_prep(c):
        slot_side, slot_rows = row_slot(r)
        return pltpu.make_async_remote_copy(
            prep, coef.at[d, :, :, slot_side, slot_rows, :], prep_sem.at[c], coef_sem.at[d],
            device_id=(chain_depth(c), chain_row(c)), device_id_type=MESH,
        )

    def send_plane(c):
        slot_side, slot_rows = row_slot(r)
        return pltpu.make_async_remote_copy(
            prep_plane.at[c % 2], plane.at[:, :, slot_side, slot_rows, :], prep_plane_sem.at[c % 2], plane_sem,
            device_id=(chain_depth(c), chain_row(c)), device_id_type=MESH,
        )

    def send_slow(c):
        return pltpu.make_async_remote_copy(
            prep_slow, refs.at[d], prep_slow_sem.at[c], refs_sem,
            device_id=(chain_depth(c) + 1, chain_row(c)), device_id_type=MESH,
        )

    far_device = (3 + 2 * (far_c % 2), 4 * z + far_c)
    far_wanted = jnp.logical_or(d != 0, far_c < 2)
    far_plane = jnp.logical_and(at_end, far_c // 2 == first_chain // 2)

    def send_far():
        return pltpu.make_async_remote_copy(
            prep, relayed.at[d], prep_sem.at[far_c], relay_sem.at[d], device_id=far_device, device_id_type=MESH
        )

    def send_far_plane():
        return pltpu.make_async_remote_copy(
            prep_plane.at[far_c % 2], relayed_plane, prep_plane_sem.at[far_c % 2], relay_plane_sem,
            device_id=far_device, device_id_type=MESH,
        )

    passed_side, passed_rows = row_slot(4 * z + far_c)
    passed_to = (chain_depth(y), chain_row(y))

    def send_onward(depth):
        return pltpu.make_async_remote_copy(
            relayed.at[depth], coef.at[depth, :, :, passed_side, passed_rows, :], onward_sem.at[depth], coef_sem.at[depth],
            device_id=passed_to, device_id_type=MESH,
        )

    def send_onward_plane():
        return pltpu.make_async_remote_copy(
            relayed_plane, plane.at[:, :, passed_side, passed_rows, :], onward_plane_sem, plane_sem,
            device_id=passed_to, device_id_type=MESH,
        )

    def pass_plane():
        pltpu.make_async_copy(relayed_plane, relayed_plane, relay_plane_sem).wait()
        send_onward_plane().start()

    def pass_depth(depth):
        pltpu.make_async_copy(relayed.at[depth], relayed.at[depth], relay_sem.at[depth]).wait()
        send_onward(depth).start()

    relay_steps = jnp.where(y < 2, NZ, NZ - 1)

    def relay_depth(step):
        return jnp.where(y < 2, step, NZ - 1 - step)

    @pl.when(d == 0)
    def _():
        for w in range(2):
            for k in range(2):
                left, right = halves(src_ref[w, k])
                prep_plane[w, k, 0] = left
                prep_plane[w, k, 1] = right

    @pl.when(d == NZ - 1)
    def _():
        for w in range(2):
            for k in range(2):
                left, right = halves(adj_ref[w, k])
                prep_plane[w, k, 0] = left
                prep_plane[w, k, 1] = right

    greetings = 1 + jnp.where(at_end, 2, 0) + jnp.where(r == REF_ROW, 4, 0)
    greetings = greetings + jnp.where(jnp.logical_and(relay_here, jnp.logical_not(helper_here)), 1, 0)
    greetings = greetings + jnp.where(edge_here, 4, 0)
    greetings = jnp.where(chain_here, 7, jnp.where(helper_here, 256, greetings))
    pl.semaphore_wait(barrier, greetings)

    @pl.when(far_plane)
    def _():
        send_far_plane().start()

    @pl.when(at_end)
    def _():
        for w in range(2):
            @pl.when(first_chain + w != far_c)
            def _():
                send_plane(first_chain + w).start()

    @pl.when(far_wanted)
    def _():
        send_far().start()

    @pl.when(at_end)
    def _():
        for w in range(2):
            @pl.when(first_chain + w != far_c)
            def _():
                send_prep(first_chain + w).start()

    @pl.when(r == REF_ROW)
    def _():
        @pl.loop(0, 4)
        def _(c):
            send_slow(c).start()

    @pl.when(jnp.logical_and(relay_here, jnp.logical_not(helper_here)))
    def _():
        pass_plane()

        @pl.loop(0, relay_steps)
        def _(step):
            pass_depth(relay_depth(step))

    @pl.when(jnp.logical_or(chip_here, edge_here))
    def _():
        @pl.loop(0, 4)
        def _(c):
            @pl.when(jnp.logical_and(c != far_c, jnp.logical_not(jnp.logical_and(chain_here, c == me_c))))
            def _():
                send_prep(c).start()

    @pl.when(jnp.logical_not(jnp.logical_or(chip_here, edge_here)))
    def _():
        start = jnp.where(d >= NZ // 2, 2, 0)

        @pl.loop(0, 4)
        def _(i):
            c = lax.rem(i + start, 4)
            asked = jnp.logical_and(d != 0, jnp.logical_or(d != NZ - 1, c < 2))

            @pl.when(jnp.logical_and(asked, c != far_c))
            def _():
                pl.semaphore_wait(ask_sem.at[c], 1)
                send_prep(c).start()

    def spread(step, row):
        source = me_c < 2
        target = jnp.where(source, step, NZ - 2 - step)
        to_side = row // 16
        block = jnp.where(to_side == 1, 31 - row, row)
        block = shipped.at[step, :, :, to_side, block // 4, block % 4]
        here = jnp.logical_and(target == d, row == r)

        @pl.when(here)
        def _():
            pltpu.make_async_copy(block, arrived.at[me_c], spread_sem.at[step]).start()

        @pl.when(jnp.logical_not(here))
        def _():
            pltpu.make_async_remote_copy(
                block, arrived.at[me_c], spread_sem.at[step], arrived_sem.at[me_c],
                device_id=(target, row), device_id_type=MESH,
            ).start()

    my_steps = jnp.where(me_c < 2, NZ, NZ - 1)

    @pl.when(edge_here)
    def _():
        pl.semaphore_wait(ready_sem, 1)

        @pl.loop(0, my_steps)
        def _(step):
            pltpu.make_async_copy(shipped.at[step, 0, 0], shipped.at[step, 0, 0], landed_sem.at[step]).wait()

            @pl.loop(0, 8)
            def _(i):
                spread(step, 4 * i + y)

        @pl.loop(0, my_steps)
        def _(step):
            pltpu.make_async_copy(shipped.at[step, 0, 0], shipped.at[step, 0, 0], spread_sem.at[step]).wait()

    def scale_power(depth):
        return (14 * depth) % 16, (14 * depth + 7) % 16

    def run_helper():
        source = me_c < 2
        omega = omega_ref[me_c % 2]
        steps = my_steps
        depth_of = relay_depth

        def ask(step):
            depth = depth_of(step)

            @pl.when(step < steps)
            def _():
                @pl.loop(0, NROW)
                def _(i):
                    @pl.when(jnp.logical_not(jnp.logical_or(unasked(depth, i), i % 4 == far_c)))
                    def _():
                        pl.semaphore_signal(ask_sem.at[me_c], inc=1, device_id=(depth, i), device_id_type=MESH)

        for other in (1, 3):
            pl.semaphore_signal(ready_sem, inc=1, device_id=(d, 8 * me_c + (me_c + other) % 4), device_id_type=MESH)
        ask(1)
        ask(2)
        pass_plane()
        pltpu.make_async_copy(refs, refs, refs_sem).wait()
        unit = 2.0 * math.pi / (2 * HALF)

        def send_phase(depth):
            return pltpu.make_async_remote_copy(
                phase.at[depth], phase.at[depth], phase_out_sem.at[depth], phase_sem.at[depth],
                device_id=(d - 1, r), device_id_type=MESH,
            )

        @pl.loop(0, steps)
        def _(step):
            depth = depth_of(step)
            speed = refs[depth, 0:1, 0:1] * omega
            speed2 = speed * speed
            forward_power, inverse_power = scale_power(depth)
            power = (forward_power + inverse_power).astype(f32)
            gain = jnp.exp2(jnp.full((1, 1), 1.0, f32) * power * (-0.125))

            def phase_tile(row, col, row_odd, col_odd):
                gains = gain * jnp.where(row == 0, 0.5, 1.0) * jnp.where(col == 0, 0.5, 1.0)
                row = jnp.where(row == 0, HALF, row) if row_odd else row
                col = jnp.where(col == 0, HALF, col) if col_odd else col
                wave_x, wave_y = row.astype(f32) * unit, col.astype(f32) * unit
                squared = speed2 - wave_x * wave_x - wave_y * wave_y
                damping = jnp.exp(-jnp.sqrt(jnp.maximum(-squared, 0.0))) * gains
                inside = jnp.maximum(squared, 0.0)
                angle = jnp.sqrt(inside)
                return damping * series(inside, COS_PHASE), damping * (series(inside, SIN_PHASE) * angle)

            @pl.loop(0, HALF // 8)
            def _(i):
                rows = pl.ds(pl.multiple_of(i * 8, 8), 8)
                row = iota2((8, HALF), 0) + i * 8
                col = iota2((8, HALF), 1)
                even = phase_tile(row, col, False, False)
                odd = phase_tile(row[:, :128], col[:, :128], False, True)
                for k in range(2):
                    for p in range(2):
                        phase[depth, 0, p, k, rows, :] = even[k]
                        phase[depth, 1, p, k, rows, 0:128] = odd[k]
                        phase[depth, 1, p, k, rows, 128:256] = even[k][:, 128:]

            row, col = iota2((8, HALF), 0), iota2((8, HALF), 1)
            for q in range(2):
                tile = phase_tile(row, col, True, q == 1)
                for k in range(2):
                    phase[depth, q, 1, k, 0:8, :] = tile[k]

            send_phase(depth).start()
            pass_depth(depth)

        @pl.loop(0, steps)
        def _(step):
            pltpu.make_async_copy(shipped.at[step], shipped.at[step], landed_sem.at[step]).wait()
            ask(step + 3)

            @pl.loop(0, 16)
            def _(i):
                spread(step, 4 * (i // 2) + (y + 2 * (i % 2)) % 4)

        @pl.loop(0, steps)
        def _(step):
            send_phase(depth_of(step)).wait_send()
            pltpu.make_async_copy(shipped.at[step, 0], shipped.at[step, 0], spread_sem.at[step]).wait()

    def run_chain(source):
        w = me_c % 2
        omega = omega_ref[w]

        def depth_of(step):
            return step if source else NZ - 1 - step

        for p in range(2):
            for dest, dims in ((base, (0, 1)), (base_t, (1, 0))):
                n = iota2((HALF, HALF), dims[0])
                k = iota2((HALF, HALF), dims[1])
                if p == 1:
                    k = jnp.where(k == 0, HALF, k)
                angle = ((2 * n + 1) * k % (4 * HALF)).astype(f32) * (2.0 * math.pi / (4 * HALF))
                dest[p] = (jnp.cos(angle) if p == 0 else jnp.sin(angle)) * 0.0625
            row, col = iota2((HALF, HALF), 0), iota2((HALF, HALF), 1)
            near = jnp.where(jnp.abs(row - col) == 1, 1.0, jnp.where(row == col, -2.0, 0.0))
            corner = jnp.logical_and(row == col, jnp.logical_or(row == 0, row == HALF - 1))
            ridge[p] = jnp.where(corner, -1.0 if p == 0 else -3.0, near).astype(bf16)

        slot_side, slot_rows = row_slot(r)
        own = pltpu.make_async_copy(prep, coef.at[d, :, :, slot_side, slot_rows, :], coef_sem.at[d])
        own.start()

        def make_tables(depth):
            forward_power, inverse_power = scale_power(depth)
            for way, power in enumerate((forward_power, inverse_power)):
                scale = jnp.exp2(jnp.full((1, 1), 1.0, f32) * power.astype(f32) * 0.0625)
                for p in range(2):
                    table[way, p] = (base[p] * scale).astype(bf16)
                    table_t[way, p] = (base_t[p] * scale).astype(bf16)

        def propagate(depth):
            pltpu.make_async_copy(phase.at[depth], phase.at[depth], phase_sem.at[depth]).wait()
            for q in range(2):
                for p in range(2):
                    half = dot(xb[q, p].reshape(2 * HALF, HALF), table[0, q]).astype(bf16)
                    real = dot(table_t[0, p], half[:HALF])
                    imag = dot(table_t[0, p], half[HALF:])
                    cos = phase[depth, q, p, 0]
                    sin = phase[depth, q, p, 1]
                    if source:
                        turned = (real * cos - imag * sin, real * sin + imag * cos)
                    else:
                        turned = (real * cos + imag * sin, imag * cos - real * sin)
                    back = [dot(table[1, p], part.astype(bf16)).astype(bf16) for part in turned]
                    for k in range(2):
                        eb[q, p, k] = dot(back[k], table_t[1, q])

        def laplace(blocks, q, p, k):
            values = blocks[q, p, k]
            return dot(values, ridge[q]) + dot(ridge[p], values)

        def unfold(parts):
            mixed = [[parts[q][0] + parts[q][1], parts[q][0] - parts[q][1]] for q in range(2)]
            return [[mixed[0][a] + mixed[1][a] for a in range(2)], [mixed[0][a] - mixed[1][a] for a in range(2)]]

        def tiles(body):
            @pl.loop(0, HALF // ROWS)
            def _(i):
                rows = pl.ds(pl.multiple_of(i * ROWS, ROWS), ROWS)
                for j in range(2):
                    body(i, rows, pl.ds(j * 128, 128))

        def lens_of(depth, b, a, rows, cols):
            angle = coef[depth, 0, b, a, rows, cols].astype(f32) * omega
            square = angle * angle
            return series(square, COS_LENS), series(square, SIN_LENS) * angle

        def to_helper(step):
            return pltpu.make_async_remote_copy(
                shipped.at[step], shipped.at[step], ship_sem.at[step], landed_sem.at[step],
                device_id=(d + 1, r), device_id_type=MESH,
            )

        def ship(step):
            for other in (1, 3):
                to_y = (y + other) % 4
                for a, block_y in ((0, to_y), (1, 3 - to_y)):
                    part = shipped.at[step, :, :, a, :, block_y]
                    pltpu.make_async_remote_copy(
                        part, part, edge_sem.at[step], landed_sem.at[step],
                        device_id=(d + 1, 4 * z + to_y), device_id_type=MESH,
                    ).start()
            to_helper(step).start()

        def wait_coef(depth):
            pltpu.make_async_copy(coef.at[depth], coef.at[depth], coef_sem.at[depth]).wait()

        steps = NZ if source else NZ - 1
        pltpu.make_async_copy(plane, plane, plane_sem).wait()

        def first_fold(i, rows, cols):
            for k in range(2):
                folded = unfold([[plane[k, b, a, rows, cols].astype(f32) for a in range(2)] for b in range(2)])
                for q in range(2):
                    for p in range(2):
                        if source:
                            xb[q, p, k, rows, cols] = folded[q][p].astype(bf16)
                        else:
                            eb[q, p, k, rows, cols] = folded[q][p] * 0.25
                            gb[q, p, k, rows, cols] = (folded[q][p] * 0.25).astype(bf16)

        tiles(first_fold)

        if source:
            @pl.loop(0, steps)
            def _(step):
                depth = depth_of(step)
                make_tables(depth)
                propagate(depth)
                wait_coef(depth)

                def spatial(i, rows, cols):
                    real = unfold([[eb[q, p, 0, rows, cols] for p in range(2)] for q in range(2)])
                    imag = unfold([[eb[q, p, 1, rows, cols] for p in range(2)] for q in range(2)])
                    lensed = [[[None, None], [None, None]] for _ in range(2)]
                    scaled = [[[None, None], [None, None]] for _ in range(2)]
                    for b in range(2):
                        for a in range(2):
                            cos, sin = lens_of(depth, b, a, rows, cols)
                            factor = coef[depth, 1, b, a, rows, cols].astype(f32)
                            lensed[0][b][a] = real[b][a] * cos - imag[b][a] * sin
                            lensed[1][b][a] = real[b][a] * sin + imag[b][a] * cos
                            for k in range(2):
                                scaled[k][b][a] = lensed[k][b][a] * factor
                    for k in range(2):
                        wave, bend = unfold(lensed[k]), unfold(scaled[k])
                        for q in range(2):
                            for p in range(2):
                                wb[q, p, k, rows, cols] = wave[q][p]
                                gb[q, p, k, rows, cols] = bend[q][p].astype(bf16)

                tiles(spatial)
                for q in range(2):
                    new = []
                    for p in range(2):
                        real = wb[q, p, 0] - laplace(gb, q, p, 1)
                        imag = wb[q, p, 1] + laplace(gb, q, p, 0)
                        xb[q, p, 0] = real.astype(bf16)
                        xb[q, p, 1] = imag.astype(bf16)
                        new.append((real * 0.25, imag * 0.25))
                    for k in range(2):
                        shipped[step, q, k, 0] = (new[0][k] + new[1][k]).astype(bf16).reshape(4, 4, ROWS, HALF)
                        shipped[step, q, k, 1] = (new[0][k] - new[1][k]).astype(bf16).reshape(4, 4, ROWS, HALF)
                ship(step)
        else:
            @pl.loop(0, steps)
            def _(step):
                depth = depth_of(step)
                make_tables(depth)
                for q in range(2):
                    for p in range(2):
                        for k in range(2):
                            wb[q, p, k] = laplace(gb, q, p, k)
                wait_coef(depth)

                def spatial(i, rows, cols):
                    value = [unfold([[eb[q, p, k, rows, cols] for p in range(2)] for q in range(2)]) for k in range(2)]
                    bend = [unfold([[wb[q, p, k, rows, cols] for p in range(2)] for q in range(2)]) for k in range(2)]
                    pulled = [[[None, None], [None, None]] for _ in range(2)]
                    for b in range(2):
                        for a in range(2):
                            cos, sin = lens_of(depth, b, a, rows, cols)
                            factor = coef[depth, 1, b, a, rows, cols].astype(f32)
                            real = value[0][b][a] + factor * bend[1][b][a]
                            imag = value[1][b][a] - factor * bend[0][b][a]
                            pulled[0][b][a] = real * cos + imag * sin
                            pulled[1][b][a] = imag * cos - real * sin
                    for k in range(2):
                        folded = unfold(pulled[k])
                        for q in range(2):
                            for p in range(2):
                                xb[q, p, k, rows, cols] = folded[q][p].astype(bf16)

                tiles(spatial)
                propagate(depth)

                def finish(i, rows, cols):
                    for q in range(2):
                        for k in range(2):
                            even, odd = eb[q, 0, k, rows, cols], eb[q, 1, k, rows, cols]
                            gb[q, 0, k, rows, cols] = even.astype(bf16)
                            gb[q, 1, k, rows, cols] = odd.astype(bf16)
                            shipped[step, q, k, 0, i // 4, i % 4, :, cols] = (even + odd).astype(bf16)
                            shipped[step, q, k, 1, i // 4, i % 4, :, cols] = (even - odd).astype(bf16)

                tiles(finish)
                ship(step)

        @pl.loop(0, steps)
        def _(step):
            to_helper(step).wait_send()
            pltpu.make_async_copy(shipped.at[step, 0], shipped.at[step, 0], edge_sem.at[step]).wait()

    @pl.when(helper_here)
    def _():
        run_helper()

    @pl.when(jnp.logical_and(chain_here, me_c < 2))
    def _():
        run_chain(True)

    @pl.when(jnp.logical_and(chain_here, me_c >= 2))
    def _():
        run_chain(False)

    def arrival(c):
        kept = jnp.logical_and(jnp.logical_or(helper_here, edge_here), me_c == c)

        @pl.when(jnp.logical_not(kept))
        def _():
            pltpu.make_async_copy(arrived.at[c], arrived.at[c], arrived_sem.at[c]).wait()

    for c in range(2):
        arrival(c)

    @pl.when(d != NZ - 1)
    def _():
        for c in range(2, 4):
            arrival(c)

    last = d == NZ - 1
    total = [None, None]
    for w in range(2):
        below = [[arrived[w, q, k].astype(f32) for k in range(2)] for q in range(2)]
        above = [[arrived[2 + w, q, k].astype(f32) for k in range(2)] for q in range(2)]
        for b in range(2):
            sign = 1.0 if b == 0 else -1.0
            down = [below[0][k] + sign * below[1][k] for k in range(2)]
            up = [
                jnp.where(last, prep_plane[w, k, b].astype(f32), above[0][k] + sign * above[1][k])
                for k in range(2)
            ]
            term = omega_ref[w] * (down[0] * up[1] - down[1] * up[0])
            total[b] = term if total[b] is None else total[b] + term
    exact = lax.Precision.HIGHEST
    total = [dot(turn, part, exact) for part in total]
    out_ref[:, :HALF] = total[0]
    out_ref[:, HALF:] = dot(total[1], exchange(HALF), exact)

    @pl.loop(0, 4)
    def _(c):
        sent = jnp.logical_and(jnp.logical_not(jnp.logical_and(chain_here, me_c == c)), jnp.logical_or(d != 0, c < 2))

        @pl.when(sent)
        def _():
            send_prep(c).wait_send()

        @pl.when(r == REF_ROW)
        def _():
            send_slow(c).wait_send()

    @pl.when(at_end)
    def _():
        for w in range(2):
            send_plane(first_chain + w).wait_send()

    @pl.when(relay_here)
    def _():
        send_onward_plane().wait_send()

        @pl.loop(0, relay_steps)
        def _(step):
            send_onward(relay_depth(step)).wait_send()


def per_device(source_top, adjoint_bottom, slowness, correction, slowness_ref, omega):
    vmem = pl.BlockSpec(memory_space=pltpu.VMEM)
    smem = pl.BlockSpec(memory_space=pltpu.SMEM)
    dma, plain = pltpu.SemaphoreType.DMA, pltpu.SemaphoreType.REGULAR
    block = (HALF, HALF)
    gradient = pl.pallas_call(
        kernel,
        out_shape=jax.ShapeDtypeStruct((ROWS, 2 * HALF), f32),
        in_specs=[vmem, vmem, vmem, vmem, smem, smem],
        out_specs=vmem,
        scratch_shapes=[
            pltpu.VMEM((2, 2, ROWS, HALF), bf16),
            pltpu.VMEM((2, 2, 2, ROWS, HALF), bf16),
            pltpu.VMEM((8, 128), f32),
            pltpu.VMEM((NZ, 2, 2, 2) + block, bf16),
            pltpu.VMEM((2, 2, 2) + block, bf16),
            pltpu.VMEM((NZ, 8, 128), f32),
            pltpu.VMEM((4, 2, 2, ROWS, HALF), bf16),
            pltpu.VMEM((NZ, 2, 2, 2) + block, f32),
            pltpu.VMEM((2,) + block, f32),
            pltpu.VMEM((2,) + block, f32),
            pltpu.VMEM((2, 2) + block, bf16),
            pltpu.VMEM((2, 2) + block, bf16),
            pltpu.VMEM((2,) + block, bf16),
            pltpu.VMEM((NZ, 2, 2, 2, 4, 4, ROWS, HALF), bf16),
            pltpu.VMEM((2, 2, 2) + block, bf16),
            pltpu.VMEM((2, 2, 2) + block, bf16),
            pltpu.VMEM((2, 2, 2) + block, f32),
            pltpu.VMEM((2, 2, 2) + block, f32),
            dma((4,)),
            dma((2,)),
            dma((4,)),
            dma((NZ,)),
            dma(()),
            dma(()),
            dma((4,)),
            dma((NZ,)),
            plain((4,)),
            dma((NZ,)),
            dma((NZ,)),
            dma((NZ,)),
            dma((NZ,)),
            dma((NZ,)),
            plain(()),
            pltpu.VMEM((NZ, 2, 2, ROWS, HALF), bf16),
            pltpu.VMEM((2, 2, ROWS, HALF), bf16),
            dma((NZ,)),
            dma(()),
            dma((NZ,)),
            dma(()),
        ],
        compiler_params=pltpu.CompilerParams(
            collective_id=0, has_side_effects=True, vmem_limit_bytes=60 * 1024 * 1024
        ),
        name="imaging",
    )(slowness, correction, source_top, adjoint_bottom, slowness_ref, omega)
    return gradient[None]


def solution(mesh):
    in_specs = (
        P(None, None, "rows", None),
        P(None, None, "rows", None),
        P("depth", "rows", None),
        P("depth", "rows", None),
        P("depth"),
        P(),
    )
    return jax.shard_map(
        per_device, mesh=mesh, in_specs=in_specs, out_specs=P("depth", "rows", None), check_vma=False
    )
```

```python
import math

import jax
import jax.numpy as jnp
import numpy as np
from jax import lax
from jax.experimental import pallas as pl
from jax.experimental.pallas import tpu as pltpu
from jax.sharding import PartitionSpec as P

MESH = pl.DeviceIdType.MESH
f32, bf16 = jnp.float32, jnp.bfloat16
HALF = 256
ROWS = 16
NROW = 32
NZ = 8
REF_ROW = 5


def chain_depth(c):
    return 2 + 2 * (c % 2)


def chain_row(c):
    return 9 * c


def on_chain_chip(d, r):
    return jnp.logical_and(r % 9 == 0, d // 2 == 1 + (r // 9) % 2)


def on_edge(d, r):
    c = r // 8
    even = jnp.logical_and((r // 4) % 2 == 0, (r + c) % 2 == 1)
    return jnp.logical_and(even, d == 3 + 2 * (c % 2))


def unasked(d, r):
    return jnp.logical_or(on_chain_chip(d, r), on_edge(d, r))


def dot(a, b, precision=None):
    return jnp.dot(a, b, preferred_element_type=f32, precision=precision)


def iota2(shape, dim):
    return lax.broadcasted_iota(jnp.int32, shape, dim)


def exchange(size, flipped=True):
    row, col = iota2((size, size), 0), iota2((size, size), 1)
    target = jnp.where(flipped, size - 1 - row, row)
    return jnp.where(col == target, 1.0, 0.0).astype(f32)


def series(t, coefs):
    total = t * coefs[-1] + coefs[-2]
    for coef in coefs[-3::-1]:
        total = total * t + coef
    return total


LENS_REACH = 0.42


def fitted(function, reach):
    fit = np.polynomial.Chebyshev.interpolate(lambda t: function(np.sqrt(np.maximum(t, 1e-30))), 3, domain=(0.0, reach))
    return [float(coef) for coef in fit.convert(kind=np.polynomial.Polynomial).coef]


COS_LENS = fitted(np.cos, LENS_REACH)
SIN_LENS = fitted(lambda a: np.sin(a) / a, LENS_REACH)
COS_PHASE = [(-1.0) ** k / math.factorial(2 * k) for k in range(9)]
SIN_PHASE = [(-1.0) ** k / math.factorial(2 * k + 1) for k in range(8)]


def row_slot(r):
    side = r // 16
    block = jnp.where(side == 1, 31 - r, r)
    return side, pl.ds(pl.multiple_of(block * ROWS, ROWS), ROWS)


def kernel(
    slow_ref, corr_ref, src_ref, adj_ref, ref_ref, omega_ref, out_ref,
    prep, prep_plane, prep_slow,
    coef, plane, refs, arrived,
    phase, base, base_t, table, table_t, ridge,
    shipped, xb, yb, gb, eb, wb,
    prep_sem, prep_plane_sem, prep_slow_sem,
    coef_sem, plane_sem, refs_sem, arrived_sem, ship_sem, ask_sem, landed_sem, spread_sem, phase_sem, phase_out_sem,
    edge_sem, ready_sem, relayed, relayed_plane, relay_sem, relay_plane_sem, onward_sem, onward_plane_sem,
):
    d = lax.axis_index("depth")
    r = lax.axis_index("rows")
    side = r // 16
    barrier = pltpu.get_barrier_semaphore()
    z, y = r // 4, r % 4
    me_c = z // 2
    chip_here = on_chain_chip(d, r)
    chain_here = jnp.logical_and(chip_here, d % 2 == 0)
    helper_here = jnp.logical_and(chip_here, d % 2 == 1)
    edge_here = on_edge(d, r)
    relay_here = d == 3 + 2 * (y % 2)
    at_end = jnp.logical_or(d == 0, d == NZ - 1)
    first_chain = jnp.where(d == 0, 0, 2)
    far_c = (y + 2) % 4

    def greet(depth, row):
        pl.semaphore_signal(barrier, inc=1, device_id=(depth, row), device_id_type=MESH)

    @pl.when(chain_here)
    def _():
        first = jnp.where(me_c < 2, 0, NZ - 1)

        @pl.loop(0, NROW)
        def _(i):
            greet(first, i)

        @pl.loop(0, 8)
        def _(i):
            @pl.when(i != z)
            def _():
                greet(d + 1, 4 * i + y)

        for c in range(4):
            @pl.when(c != me_c)
            def _():
                greet(chain_depth(c), chain_row(c))
            for other in (1, 3):
                greet(chain_depth(c) + 1, 8 * c + (c + other) % 4)

    @pl.when(relay_here)
    def _():
        @pl.loop(0, NZ)
        def _(i):
            greet(i, 4 * z + far_c)

    @pl.when(helper_here)
    def _():
        greet(d - 1, r)

        @pl.loop(0, NZ)
        def _(i):
            greet(i, REF_ROW)

    @pl.when(edge_here)
    def _():
        greet(d - 1, 9 * me_c)

    for c in range(4):
        @pl.when(jnp.logical_or(d != chain_depth(c) + 1, r != chain_row(c)))
        def _():
            greet(chain_depth(c) + 1, chain_row(c))

    turn = exchange(ROWS, side == 1)
    flip = exchange(HALF).astype(bf16)
    turn_b = turn.astype(bf16)

    def halves(values):
        turned = dot(turn_b, values).astype(bf16)
        return turned[:, :HALF], dot(turned[:, HALF:], flip).astype(bf16)

    slow_value = ref_ref[0]
    for k, values in enumerate((slow_ref[0] - slow_value, corr_ref[0])):
        left, right = halves(values.astype(bf16))
        prep[k, 0] = left
        prep[k, 1] = right
    prep_slow[...] = jnp.full((8, 128), slow_value, f32)

    def send_prep(c):
        slot_side, slot_rows = row_slot(r)
        return pltpu.make_async_remote_copy(
            prep, coef.at[d, :, :, slot_side, slot_rows, :], prep_sem.at[c], coef_sem.at[d],
            device_id=(chain_depth(c), chain_row(c)), device_id_type=MESH,
        )

    def send_plane(c):
        slot_side, slot_rows = row_slot(r)
        return pltpu.make_async_remote_copy(
            prep_plane.at[c % 2], plane.at[:, :, slot_side, slot_rows, :], prep_plane_sem.at[c % 2], plane_sem,
            device_id=(chain_depth(c), chain_row(c)), device_id_type=MESH,
        )

    def send_slow(c):
        return pltpu.make_async_remote_copy(
            prep_slow, refs.at[d], prep_slow_sem.at[c], refs_sem,
            device_id=(chain_depth(c) + 1, chain_row(c)), device_id_type=MESH,
        )

    far_device = (3 + 2 * (far_c % 2), 4 * z + far_c)
    far_wanted = jnp.logical_or(d != 0, far_c < 2)
    far_plane = jnp.logical_and(at_end, far_c // 2 == first_chain // 2)

    def send_far():
        return pltpu.make_async_remote_copy(
            prep, relayed.at[d], prep_sem.at[far_c], relay_sem.at[d], device_id=far_device, device_id_type=MESH
        )

    def send_far_plane():
        return pltpu.make_async_remote_copy(
            prep_plane.at[far_c % 2], relayed_plane, prep_plane_sem.at[far_c % 2], relay_plane_sem,
            device_id=far_device, device_id_type=MESH,
        )

    passed_side, passed_rows = row_slot(4 * z + far_c)
    passed_to = (chain_depth(y), chain_row(y))

    def send_onward(depth):
        return pltpu.make_async_remote_copy(
            relayed.at[depth], coef.at[depth, :, :, passed_side, passed_rows, :], onward_sem.at[depth], coef_sem.at[depth],
            device_id=passed_to, device_id_type=MESH,
        )

    def send_onward_plane():
        return pltpu.make_async_remote_copy(
            relayed_plane, plane.at[:, :, passed_side, passed_rows, :], onward_plane_sem, plane_sem,
            device_id=passed_to, device_id_type=MESH,
        )

    def pass_plane():
        pltpu.make_async_copy(relayed_plane, relayed_plane, relay_plane_sem).wait()
        send_onward_plane().start()

    def pass_depth(depth):
        pltpu.make_async_copy(relayed.at[depth], relayed.at[depth], relay_sem.at[depth]).wait()
        send_onward(depth).start()

    relay_steps = jnp.where(y < 2, NZ, NZ - 1)

    def relay_depth(step):
        return jnp.where(y < 2, step, NZ - 1 - step)

    @pl.when(d == 0)
    def _():
        for w in range(2):
            for k in range(2):
                left, right = halves(src_ref[w, k])
                prep_plane[w, k, 0] = left
                prep_plane[w, k, 1] = right

    @pl.when(d == NZ - 1)
    def _():
        for w in range(2):
            for k in range(2):
                left, right = halves(adj_ref[w, k])
                prep_plane[w, k, 0] = left
                prep_plane[w, k, 1] = right

    greetings = 1 + jnp.where(at_end, 2, 0) + jnp.where(r == REF_ROW, 4, 0)
    greetings = greetings + jnp.where(jnp.logical_and(relay_here, jnp.logical_not(helper_here)), 1, 0)
    greetings = greetings + jnp.where(edge_here, 4, 0)
    greetings = jnp.where(chain_here, 7, jnp.where(helper_here, 256, greetings))
    pl.semaphore_wait(barrier, greetings)

    @pl.when(far_plane)
    def _():
        send_far_plane().start()

    @pl.when(at_end)
    def _():
        for w in range(2):
            @pl.when(first_chain + w != far_c)
            def _():
                send_plane(first_chain + w).start()

    @pl.when(far_wanted)
    def _():
        send_far().start()

    @pl.when(at_end)
    def _():
        for w in range(2):
            @pl.when(first_chain + w != far_c)
            def _():
                send_prep(first_chain + w).start()

    @pl.when(r == REF_ROW)
    def _():
        @pl.loop(0, 4)
        def _(c):
            send_slow(c).start()

    @pl.when(jnp.logical_and(relay_here, jnp.logical_not(helper_here)))
    def _():
        pass_plane()

        @pl.loop(0, relay_steps)
        def _(step):
            pass_depth(relay_depth(step))

    @pl.when(jnp.logical_or(chip_here, edge_here))
    def _():
        @pl.loop(0, 4)
        def _(c):
            @pl.when(jnp.logical_and(c != far_c, jnp.logical_not(jnp.logical_and(chain_here, c == me_c))))
            def _():
                send_prep(c).start()

    @pl.when(jnp.logical_not(jnp.logical_or(chip_here, edge_here)))
    def _():
        start = jnp.where(d >= NZ // 2, 2, 0)

        @pl.loop(0, 4)
        def _(i):
            c = lax.rem(i + start, 4)
            asked = jnp.logical_and(d != 0, jnp.logical_or(d != NZ - 1, c < 2))

            @pl.when(jnp.logical_and(asked, c != far_c))
            def _():
                pl.semaphore_wait(ask_sem.at[c], 1)
                send_prep(c).start()

    def spread(step, row):
        source = me_c < 2
        target = jnp.where(source, step, NZ - 2 - step)
        to_side = row // 16
        block = jnp.where(to_side == 1, 31 - row, row)
        block = shipped.at[step, :, :, to_side, block // 4, block % 4]
        here = jnp.logical_and(target == d, row == r)

        @pl.when(here)
        def _():
            pltpu.make_async_copy(block, arrived.at[me_c], spread_sem.at[step]).start()

        @pl.when(jnp.logical_not(here))
        def _():
            pltpu.make_async_remote_copy(
                block, arrived.at[me_c], spread_sem.at[step], arrived_sem.at[me_c],
                device_id=(target, row), device_id_type=MESH,
            ).start()

    my_steps = jnp.where(me_c < 2, NZ, NZ - 1)

    def ask(step):
        depth = jnp.where(me_c < 2, step, NZ - 1 - step)

        @pl.when(step < my_steps)
        def _():
            @pl.loop(0, NROW)
            def _(i):
                @pl.when(jnp.logical_not(jnp.logical_or(unasked(depth, i), i % 4 == (me_c + 2) % 4)))
                def _():
                    pl.semaphore_signal(ask_sem.at[me_c], inc=1, device_id=(depth, i), device_id_type=MESH)

    @pl.when(edge_here)
    def _():
        pl.semaphore_wait(ready_sem, 1)

        @pl.loop(0, my_steps)
        def _(step):
            pltpu.make_async_copy(shipped.at[step, 0, 0], shipped.at[step, 0, 0], landed_sem.at[step]).wait()

            @pl.when(y == (me_c + 1) % 4)
            def _():
                ask(step + 4)

            @pl.loop(0, 8)
            def _(i):
                spread(step, 4 * i + y)

        @pl.loop(0, my_steps)
        def _(step):
            pltpu.make_async_copy(shipped.at[step, 0, 0], shipped.at[step, 0, 0], spread_sem.at[step]).wait()

    def scale_power(depth):
        return (14 * depth) % 16, (14 * depth + 7) % 16

    def run_helper():
        source = me_c < 2
        omega = omega_ref[me_c % 2]
        steps = my_steps
        depth_of = relay_depth

        for other in (1, 3):
            pl.semaphore_signal(ready_sem, inc=1, device_id=(d, 8 * me_c + (me_c + other) % 4), device_id_type=MESH)
        ask(1)
        ask(2)
        ask(3)
        pass_plane()
        pltpu.make_async_copy(refs, refs, refs_sem).wait()

        unit = 2.0 * math.pi / (2 * HALF)

        def send_phase(depth):
            return pltpu.make_async_remote_copy(
                phase.at[depth], phase.at[depth], phase_out_sem.at[depth], phase_sem.at[depth],
                device_id=(d - 1, r), device_id_type=MESH,
            )

        def forward_rows(step):
            pltpu.make_async_copy(shipped.at[step], shipped.at[step], landed_sem.at[step]).wait()

            @pl.loop(0, 16)
            def _(i):
                spread(step, 4 * (i // 2) + (y + 2 * (i % 2)) % 4)

        def make_phase(step):
            depth = depth_of(step)
            speed = refs[depth, 0:1, 0:1] * omega
            speed2 = speed * speed
            forward_power, inverse_power = scale_power(depth)
            power = (forward_power + inverse_power).astype(f32)
            gain = jnp.exp2(jnp.full((1, 1), 1.0, f32) * power * (-0.125))

            def phase_tile(row, col, row_odd, col_odd):
                gains = gain * jnp.where(row == 0, 0.5, 1.0) * jnp.where(col == 0, 0.5, 1.0)
                row = jnp.where(row == 0, HALF, row) if row_odd else row
                col = jnp.where(col == 0, HALF, col) if col_odd else col
                wave_x, wave_y = row.astype(f32) * unit, col.astype(f32) * unit
                squared = speed2 - wave_x * wave_x - wave_y * wave_y
                root = jnp.sqrt(jnp.abs(squared))
                waving = squared > 0.0
                inside = jnp.where(waving, squared, 0.0)
                damping = jnp.where(waving, 1.0, jnp.exp(-root)) * gains
                sine = jnp.where(waving, series(inside, SIN_PHASE) * root, 0.0)
                return damping * series(inside, COS_PHASE), damping * sine

            @pl.loop(0, HALF // 8)
            def _(i):
                rows = pl.ds(pl.multiple_of(i * 8, 8), 8)
                row = iota2((8, HALF), 0) + i * 8
                col = iota2((8, HALF), 1)
                even = phase_tile(row, col, False, False)
                odd = phase_tile(row[:, :128], col[:, :128], False, True)
                for k in range(2):
                    for p in range(2):
                        phase[depth, 0, p, k, rows, :] = even[k]
                        phase[depth, 1, p, k, rows, 0:128] = odd[k]
                        phase[depth, 1, p, k, rows, 128:256] = even[k][:, 128:]

            row, col = iota2((8, HALF), 0), iota2((8, HALF), 1)
            for q in range(2):
                tile = phase_tile(row, col, True, q == 1)
                for k in range(2):
                    phase[depth, q, 1, k, 0:8, :] = tile[k]

            send_phase(depth).start()

        @pl.loop(-3, steps)
        def _(step):
            @pl.when(step >= 0)
            def _():
                forward_rows(step)

            @pl.when(step + 3 < steps)
            def _():
                make_phase(step + 3)

            @pl.when(step == -3)
            def _():
                @pl.loop(0, steps)
                def _(later):
                    pass_depth(depth_of(later))

        @pl.loop(0, steps)
        def _(step):
            send_phase(depth_of(step)).wait_send()
            pltpu.make_async_copy(shipped.at[step, 0], shipped.at[step, 0], spread_sem.at[step]).wait()

    def run_chain(source):
        w = me_c % 2
        omega = omega_ref[w]

        def depth_of(step):
            return step if source else NZ - 1 - step

        for p in range(2):
            for dest, dims in ((base, (0, 1)), (base_t, (1, 0))):
                n = iota2((HALF, HALF), dims[0])
                k = iota2((HALF, HALF), dims[1])
                if p == 1:
                    k = jnp.where(k == 0, HALF, k)
                angle = ((2 * n + 1) * k % (4 * HALF)).astype(f32) * (2.0 * math.pi / (4 * HALF))
                dest[p] = (jnp.cos(angle) if p == 0 else jnp.sin(angle)) * 0.0625
            row, col = iota2((HALF, HALF), 0), iota2((HALF, HALF), 1)
            near = jnp.where(jnp.abs(row - col) == 1, 1.0, jnp.where(row == col, -2.0, 0.0))
            corner = jnp.logical_and(row == col, jnp.logical_or(row == 0, row == HALF - 1))
            ridge[p] = jnp.where(corner, -1.0 if p == 0 else -3.0, near).astype(bf16)

        slot_side, slot_rows = row_slot(r)
        own = pltpu.make_async_copy(prep, coef.at[d, :, :, slot_side, slot_rows, :], coef_sem.at[d])
        own.start()

        def make_tables(depth):
            forward_power, inverse_power = scale_power(depth)
            for way, power in enumerate((forward_power, inverse_power)):
                scale = jnp.exp2(jnp.full((1, 1), 1.0, f32) * power.astype(f32) * 0.0625)
                for p in range(2):
                    table[way, p] = (base[p] * scale).astype(bf16)
                    table_t[way, p] = (base_t[p] * scale).astype(bf16)

        def propagate(depth):
            pltpu.make_async_copy(phase.at[depth], phase.at[depth], phase_sem.at[depth]).wait()
            for q in range(2):
                for p in range(2):
                    half = dot(xb[q, p].reshape(2 * HALF, HALF), table[0, q]).astype(bf16)
                    yb[q, p] = half.reshape(2, HALF, HALF)
            for p in range(2):
                for q in range(2):
                    real = dot(table_t[0, p], yb[q, p, 0])
                    imag = dot(table_t[0, p], yb[q, p, 1])
                    cos = phase[depth, q, p, 0]
                    sin = phase[depth, q, p, 1]
                    if source:
                        turned = (real * cos - imag * sin, real * sin + imag * cos)
                    else:
                        turned = (real * cos + imag * sin, imag * cos - real * sin)
                    for k in range(2):
                        yb[q, p, k] = turned[k].astype(bf16)
            for p in range(2):
                for q in range(2):
                    for k in range(2):
                        xb[q, p, k] = dot(table[1, p], yb[q, p, k]).astype(bf16)
            for q in range(2):
                for p in range(2):
                    eb[q, p] = dot(xb[q, p].reshape(2 * HALF, HALF), table_t[1, q]).reshape(2, HALF, HALF)

        def laplace(blocks, q, p, k):
            values = blocks[q, p, k]
            return dot(values, ridge[q]) + dot(ridge[p], values)

        def unfold(parts):
            mixed = [[parts[q][0] + parts[q][1], parts[q][0] - parts[q][1]] for q in range(2)]
            return [[mixed[0][a] + mixed[1][a] for a in range(2)], [mixed[0][a] - mixed[1][a] for a in range(2)]]

        def tiles(body):
            @pl.loop(0, HALF // ROWS)
            def _(i):
                rows = pl.ds(pl.multiple_of(i * ROWS, ROWS), ROWS)
                for j in range(2):
                    body(i, rows, pl.ds(j * 128, 128))

        powers = [omega]
        for _ in range(6):
            powers.append(powers[-1] * omega)
        cos_lens = [COS_LENS[0]] + [COS_LENS[k] * powers[2 * k - 1] for k in range(1, 4)]
        sin_lens = [SIN_LENS[k] * powers[2 * k] for k in range(4)]

        def lens_of(depth, b, a, rows, cols):
            offset = coef[depth, 0, b, a, rows, cols].astype(f32)
            square = offset * offset
            return series(square, cos_lens), series(square, sin_lens) * offset

        def to_helper(step):
            return pltpu.make_async_remote_copy(
                shipped.at[step], shipped.at[step], ship_sem.at[step], landed_sem.at[step],
                device_id=(d + 1, r), device_id_type=MESH,
            )

        def ship(step):
            for other in (1, 3):
                to_y = (y + other) % 4
                for a, block_y in ((0, to_y), (1, 3 - to_y)):
                    part = shipped.at[step, :, :, a, :, block_y]
                    pltpu.make_async_remote_copy(
                        part, part, edge_sem.at[step], landed_sem.at[step],
                        device_id=(d + 1, 4 * z + to_y), device_id_type=MESH,
                    ).start()
            to_helper(step).start()

        def wait_coef(depth):
            pltpu.make_async_copy(coef.at[depth], coef.at[depth], coef_sem.at[depth]).wait()

        steps = NZ if source else NZ - 1
        pltpu.make_async_copy(plane, plane, plane_sem).wait()

        def first_fold(i, rows, cols):
            for k in range(2):
                folded = unfold([[plane[k, b, a, rows, cols].astype(f32) for a in range(2)] for b in range(2)])
                for q in range(2):
                    for p in range(2):
                        if source:
                            xb[q, p, k, rows, cols] = folded[q][p].astype(bf16)
                        else:
                            eb[q, p, k, rows, cols] = folded[q][p] * 0.25
                            gb[q, p, k, rows, cols] = (folded[q][p] * 0.25).astype(bf16)

        tiles(first_fold)

        if source:
            @pl.loop(0, steps)
            def _(step):
                depth = depth_of(step)
                make_tables(depth)
                propagate(depth)
                wait_coef(depth)

                def spatial(i, rows, cols):
                    real = unfold([[eb[q, p, 0, rows, cols] for p in range(2)] for q in range(2)])
                    imag = unfold([[eb[q, p, 1, rows, cols] for p in range(2)] for q in range(2)])
                    lensed = [[[None, None], [None, None]] for _ in range(2)]
                    scaled = [[[None, None], [None, None]] for _ in range(2)]
                    for b in range(2):
                        for a in range(2):
                            cos, sin = lens_of(depth, b, a, rows, cols)
                            factor = coef[depth, 1, b, a, rows, cols].astype(f32)
                            lensed[0][b][a] = real[b][a] * cos - imag[b][a] * sin
                            lensed[1][b][a] = real[b][a] * sin + imag[b][a] * cos
                            for k in range(2):
                                scaled[k][b][a] = lensed[k][b][a] * factor
                    for k in range(2):
                        wave, bend = unfold(lensed[k]), unfold(scaled[k])
                        for q in range(2):
                            for p in range(2):
                                wb[q, p, k, rows, cols] = wave[q][p]
                                gb[q, p, k, rows, cols] = bend[q][p].astype(bf16)

                tiles(spatial)
                for q in range(2):
                    new = []
                    for p in range(2):
                        real = wb[q, p, 0] - laplace(gb, q, p, 1)
                        imag = wb[q, p, 1] + laplace(gb, q, p, 0)
                        xb[q, p, 0] = real.astype(bf16)
                        xb[q, p, 1] = imag.astype(bf16)
                        new.append((real * 0.25, imag * 0.25))
                    for k in range(2):
                        shipped[step, q, k, 0] = (new[0][k] + new[1][k]).astype(bf16).reshape(4, 4, ROWS, HALF)
                        shipped[step, q, k, 1] = (new[0][k] - new[1][k]).astype(bf16).reshape(4, 4, ROWS, HALF)
                ship(step)
        else:
            @pl.loop(0, steps)
            def _(step):
                depth = depth_of(step)
                make_tables(depth)
                for q in range(2):
                    for p in range(2):
                        for k in range(2):
                            wb[q, p, k] = laplace(gb, q, p, k)
                wait_coef(depth)

                def spatial(i, rows, cols):
                    value = [unfold([[eb[q, p, k, rows, cols] for p in range(2)] for q in range(2)]) for k in range(2)]
                    bend = [unfold([[wb[q, p, k, rows, cols] for p in range(2)] for q in range(2)]) for k in range(2)]
                    pulled = [[[None, None], [None, None]] for _ in range(2)]
                    for b in range(2):
                        for a in range(2):
                            cos, sin = lens_of(depth, b, a, rows, cols)
                            factor = coef[depth, 1, b, a, rows, cols].astype(f32)
                            real = value[0][b][a] + factor * bend[1][b][a]
                            imag = value[1][b][a] - factor * bend[0][b][a]
                            pulled[0][b][a] = real * cos + imag * sin
                            pulled[1][b][a] = imag * cos - real * sin
                    for k in range(2):
                        folded = unfold(pulled[k])
                        for q in range(2):
                            for p in range(2):
                                xb[q, p, k, rows, cols] = folded[q][p].astype(bf16)

                tiles(spatial)
                propagate(depth)

                def finish(i, rows, cols):
                    for q in range(2):
                        for k in range(2):
                            even, odd = eb[q, 0, k, rows, cols], eb[q, 1, k, rows, cols]
                            gb[q, 0, k, rows, cols] = even.astype(bf16)
                            gb[q, 1, k, rows, cols] = odd.astype(bf16)
                            shipped[step, q, k, 0, i // 4, i % 4, :, cols] = (even + odd).astype(bf16)
                            shipped[step, q, k, 1, i // 4, i % 4, :, cols] = (even - odd).astype(bf16)

                tiles(finish)
                ship(step)

        @pl.loop(0, steps)
        def _(step):
            to_helper(step).wait_send()
            pltpu.make_async_copy(shipped.at[step, 0], shipped.at[step, 0], edge_sem.at[step]).wait()

    @pl.when(helper_here)
    def _():
        run_helper()

    @pl.when(jnp.logical_and(chain_here, me_c < 2))
    def _():
        run_chain(True)

    @pl.when(jnp.logical_and(chain_here, me_c >= 2))
    def _():
        run_chain(False)

    def arrival(c):
        kept = jnp.logical_and(jnp.logical_or(helper_here, edge_here), me_c == c)

        @pl.when(jnp.logical_not(kept))
        def _():
            pltpu.make_async_copy(arrived.at[c], arrived.at[c], arrived_sem.at[c]).wait()

    for c in range(2):
        arrival(c)

    @pl.when(d != NZ - 1)
    def _():
        for c in range(2, 4):
            arrival(c)

    last = d == NZ - 1
    total = [None, None]
    for w in range(2):
        below = [[arrived[w, q, k].astype(f32) for k in range(2)] for q in range(2)]
        above = [[arrived[2 + w, q, k].astype(f32) for k in range(2)] for q in range(2)]
        for b in range(2):
            sign = 1.0 if b == 0 else -1.0
            down = [below[0][k] + sign * below[1][k] for k in range(2)]
            up = [
                jnp.where(last, prep_plane[w, k, b].astype(f32), above[0][k] + sign * above[1][k])
                for k in range(2)
            ]
            term = omega_ref[w] * (down[0] * up[1] - down[1] * up[0])
            total[b] = term if total[b] is None else total[b] + term
    exact = lax.Precision.HIGHEST
    total = [dot(turn, part, exact) for part in total]
    out_ref[:, :HALF] = total[0]
    out_ref[:, HALF:] = dot(total[1], exchange(HALF), exact)

    @pl.loop(0, 4)
    def _(c):
        sent = jnp.logical_and(jnp.logical_not(jnp.logical_and(chain_here, me_c == c)), jnp.logical_or(d != 0, c < 2))

        @pl.when(sent)
        def _():
            send_prep(c).wait_send()

        @pl.when(r == REF_ROW)
        def _():
            send_slow(c).wait_send()

    @pl.when(at_end)
    def _():
        for w in range(2):
            send_plane(first_chain + w).wait_send()

    @pl.when(relay_here)
    def _():
        send_onward_plane().wait_send()

        @pl.loop(0, relay_steps)
        def _(step):
            send_onward(relay_depth(step)).wait_send()


def per_device(source_top, adjoint_bottom, slowness, correction, slowness_ref, omega):
    vmem = pl.BlockSpec(memory_space=pltpu.VMEM)
    smem = pl.BlockSpec(memory_space=pltpu.SMEM)
    dma, plain = pltpu.SemaphoreType.DMA, pltpu.SemaphoreType.REGULAR
    block = (HALF, HALF)
    gradient = pl.pallas_call(
        kernel,
        out_shape=jax.ShapeDtypeStruct((ROWS, 2 * HALF), f32),
        in_specs=[vmem, vmem, vmem, vmem, smem, smem],
        out_specs=vmem,
        scratch_shapes=[
            pltpu.VMEM((2, 2, ROWS, HALF), bf16),
            pltpu.VMEM((2, 2, 2, ROWS, HALF), bf16),
            pltpu.VMEM((8, 128), f32),
            pltpu.VMEM((NZ, 2, 2, 2) + block, bf16),
            pltpu.VMEM((2, 2, 2) + block, bf16),
            pltpu.VMEM((NZ, 8, 128), f32),
            pltpu.VMEM((4, 2, 2, ROWS, HALF), bf16),
            pltpu.VMEM((NZ, 2, 2, 2) + block, f32),
            pltpu.VMEM((2,) + block, f32),
            pltpu.VMEM((2,) + block, f32),
            pltpu.VMEM((2, 2) + block, bf16),
            pltpu.VMEM((2, 2) + block, bf16),
            pltpu.VMEM((2,) + block, bf16),
            pltpu.VMEM((NZ, 2, 2, 2, 4, 4, ROWS, HALF), bf16),
            pltpu.VMEM((2, 2, 2) + block, bf16),
            pltpu.VMEM((2, 2, 2) + block, bf16),
            pltpu.VMEM((2, 2, 2) + block, bf16),
            pltpu.VMEM((2, 2, 2) + block, f32),
            pltpu.VMEM((2, 2, 2) + block, f32),
            dma((4,)),
            dma((2,)),
            dma((4,)),
            dma((NZ,)),
            dma(()),
            dma(()),
            dma((4,)),
            dma((NZ,)),
            plain((4,)),
            dma((NZ,)),
            dma((NZ,)),
            dma((NZ,)),
            dma((NZ,)),
            dma((NZ,)),
            plain(()),
            pltpu.VMEM((NZ, 2, 2, ROWS, HALF), bf16),
            pltpu.VMEM((2, 2, ROWS, HALF), bf16),
            dma((NZ,)),
            dma(()),
            dma((NZ,)),
            dma(()),
        ],
        compiler_params=pltpu.CompilerParams(
            collective_id=0, has_side_effects=True, vmem_limit_bytes=60 * 1024 * 1024
        ),
        name="imaging",
    )(slowness, correction, source_top, adjoint_bottom, slowness_ref, omega)
    return gradient[None]


def solution(mesh):
    in_specs = (
        P(None, None, "rows", None),
        P(None, None, "rows", None),
        P("depth", "rows", None),
        P("depth", "rows", None),
        P("depth"),
        P(),
    )
    return jax.shard_map(
        per_device, mesh=mesh, in_specs=in_specs, out_specs=P("depth", "rows", None), check_vma=False
    )
```

```python
import math

import jax
import jax.numpy as jnp
import numpy as np
from jax import lax
from jax.experimental import pallas as pl
from jax.experimental.pallas import tpu as pltpu
from jax.sharding import PartitionSpec as P

MESH = pl.DeviceIdType.MESH
f32, bf16 = jnp.float32, jnp.bfloat16
HALF = 256
ROWS = 16
NROW = 32
NZ = 8
REF_ROW = 5
FIRST_ROW = 6


def chain_depth(c):
    return 2 + 2 * (c % 2)


def chain_row(c):
    return 9 * c


def on_chain_chip(d, r):
    return jnp.logical_and(r % 9 == 0, d // 2 == 1 + (r // 9) % 2)


def on_edge(d, r):
    c = r // 8
    even = jnp.logical_and((r // 4) % 2 == 0, (r + c) % 2 == 1)
    return jnp.logical_and(even, d == 3 + 2 * (c % 2))


def unasked(d, r):
    return jnp.logical_or(on_chain_chip(d, r), on_edge(d, r))


def dot(a, b, precision=None):
    return jnp.dot(a, b, preferred_element_type=f32, precision=precision)


def iota2(shape, dim):
    return lax.broadcasted_iota(jnp.int32, shape, dim)


def exchange(size, flipped=True):
    row, col = iota2((size, size), 0), iota2((size, size), 1)
    target = jnp.where(flipped, size - 1 - row, row)
    return jnp.where(col == target, 1.0, 0.0).astype(f32)


def series(t, coefs):
    total = t * coefs[-1] + coefs[-2]
    for coef in coefs[-3::-1]:
        total = total * t + coef
    return total


LENS_REACH = 0.42


def fitted(function, reach):
    fit = np.polynomial.Chebyshev.interpolate(lambda t: function(np.sqrt(np.maximum(t, 1e-30))), 3, domain=(0.0, reach))
    return [float(coef) for coef in fit.convert(kind=np.polynomial.Polynomial).coef]


COS_LENS = fitted(np.cos, LENS_REACH)
SIN_LENS = fitted(lambda a: np.sin(a) / a, LENS_REACH)
COS_PHASE = [(-1.0) ** k / math.factorial(2 * k) for k in range(9)]
SIN_PHASE = [(-1.0) ** k / math.factorial(2 * k + 1) for k in range(8)]


def row_slot(r):
    side = r // 16
    block = jnp.where(side == 1, 31 - r, r)
    return side, block


def kernel(
    slow_ref, corr_ref, src_ref, adj_ref, ref_ref, omega_ref, out_ref,
    prep, prep_plane, prep_slow,
    coef, plane, refs, arrived,
    phase, base, base_t, table, table_t, ridge,
    shipped, xb, yb, gb, eb, wb,
    prep_sem, prep_plane_sem, prep_slow_sem,
    coef_sem, plane_sem, refs_sem, arrived_sem, ship_sem, ask_sem, landed_sem, spread_sem, phase_sem, phase_out_sem,
    first_slow_sem, ready_sem, relayed, relay_sem, onward_sem,
):
    d = lax.axis_index("depth")
    r = lax.axis_index("rows")
    side = r // 16
    barrier = pltpu.get_barrier_semaphore()
    z, y = r // 4, r % 4
    me_c = z // 2
    chip_here = on_chain_chip(d, r)
    chain_here = jnp.logical_and(chip_here, d % 2 == 0)
    helper_here = jnp.logical_and(chip_here, d % 2 == 1)
    edge_here = on_edge(d, r)
    relay_here = jnp.logical_and(d == 3 + 2 * (y % 2), z != 2 * y)
    at_end = jnp.logical_or(d == 0, d == NZ - 1)
    early = jnp.logical_or(d <= 1, d >= NZ - 2)
    first_chain = jnp.where(d <= 1, 0, 2)
    far_c = (y + 2) % 4
    far_here = z != 2 * far_c

    def direct(c):
        return jnp.logical_or(c != far_c, jnp.logical_not(far_here))

    def greet(depth, row):
        pl.semaphore_signal(barrier, inc=1, device_id=(depth, row), device_id_type=MESH)

    @pl.when(chain_here)
    def _():
        first = jnp.where(me_c < 2, 0, NZ - 1)

        second = jnp.where(me_c < 2, 1, NZ - 2)

        @pl.loop(0, NROW)
        def _(i):
            greet(first, i)

        @pl.loop(0, NROW)
        def _(i):
            greet(second, i)

        @pl.loop(0, 8)
        def _(i):
            @pl.when(i != z)
            def _():
                greet(d + 1, 4 * i + y)

        for c in range(4):
            @pl.when(c != me_c)
            def _():
                greet(chain_depth(c), chain_row(c))
            for other in (1, 3):
                greet(chain_depth(c) + 1, 8 * c + (c + other) % 4)

    @pl.when(jnp.logical_or(relay_here, helper_here))
    def _():
        @pl.loop(0, NZ)
        def _(i):
            greet(i, 4 * z + far_c)

    @pl.when(helper_here)
    def _():
        greet(d - 1, r)

        @pl.loop(0, NZ)
        def _(i):
            greet(i, REF_ROW)

    @pl.when(edge_here)
    def _():
        greet(d - 1, 9 * me_c)

    for c in range(4):
        @pl.when(jnp.logical_or(d != chain_depth(c) + 1, r != chain_row(c)))
        def _():
            greet(chain_depth(c) + 1, chain_row(c))

    turn = exchange(ROWS, side == 1)
    flip = exchange(HALF).astype(bf16)
    turn_b = turn.astype(bf16)

    def halves(values):
        turned = dot(turn_b, values).astype(bf16)
        return turned[:, :HALF], dot(turned[:, HALF:], flip).astype(bf16)

    slow_value = ref_ref[0]
    for k, values in enumerate((slow_ref[0] - slow_value, corr_ref[0])):
        left, right = halves(values.astype(bf16))
        prep[k, 0] = left
        prep[k, 1] = right
    prep_slow[...] = jnp.full((8, 128), slow_value, f32)

    def send_prep(c):
        slot_side, slot_rows = row_slot(r)
        return pltpu.make_async_remote_copy(
            prep, coef.at[d, slot_side, slot_rows], prep_sem.at[c], coef_sem.at[d],
            device_id=(chain_depth(c), chain_row(c)), device_id_type=MESH,
        )

    def send_plane(c):
        slot_side, slot_rows = row_slot(r)
        return pltpu.make_async_remote_copy(
            prep_plane.at[c % 2], plane.at[slot_side, slot_rows], prep_plane_sem.at[c % 2], plane_sem,
            device_id=(chain_depth(c), chain_row(c)), device_id_type=MESH,
        )

    def send_slow(c):
        return pltpu.make_async_remote_copy(
            prep_slow, refs.at[d], prep_slow_sem.at[c], refs_sem,
            device_id=(chain_depth(c) + 1, chain_row(c)), device_id_type=MESH,
        )

    far_device = (3 + 2 * (far_c % 2), 4 * z + far_c)
    far_wanted = jnp.logical_and(far_here, jnp.logical_or(d != 0, far_c < 2))

    def send_far():
        return pltpu.make_async_remote_copy(
            prep, relayed.at[d], prep_sem.at[far_c], relay_sem.at[d], device_id=far_device, device_id_type=MESH
        )

    def send_first_slow(w):
        return pltpu.make_async_remote_copy(
            prep_slow, refs.at[d], first_slow_sem.at[w], refs_sem,
            device_id=(chain_depth(first_chain + w), chain_row(first_chain + w)), device_id_type=MESH,
        )

    passed_side, passed_rows = row_slot(4 * z + far_c)
    passed_to = (chain_depth(y), chain_row(y))

    def send_onward(depth):
        return pltpu.make_async_remote_copy(
            relayed.at[depth], coef.at[depth, passed_side, passed_rows], onward_sem.at[depth], coef_sem.at[depth],
            device_id=passed_to, device_id_type=MESH,
        )

    def pass_depth(depth):
        pltpu.make_async_copy(relayed.at[depth], relayed.at[depth], relay_sem.at[depth]).wait()
        send_onward(depth).start()

    relay_steps = jnp.where(y < 2, NZ, NZ - 1)

    def relay_depth(step):
        return jnp.where(y < 2, step, NZ - 1 - step)

    @pl.when(d == 0)
    def _():
        for w in range(2):
            for k in range(2):
                left, right = halves(src_ref[w, k])
                prep_plane[w, k, 0] = left
                prep_plane[w, k, 1] = right

    @pl.when(d == NZ - 1)
    def _():
        for w in range(2):
            for k in range(2):
                left, right = halves(adj_ref[w, k])
                prep_plane[w, k, 0] = left
                prep_plane[w, k, 1] = right

    greetings = 1 + jnp.where(early, 2, 0) + jnp.where(r == REF_ROW, 4, 0)
    greetings = greetings + jnp.where(relay_here, 1, 0)
    greetings = greetings + jnp.where(edge_here, 4, 0)
    greetings = jnp.where(chain_here, 7, jnp.where(helper_here, 256, greetings))
    def scale_power(depth):
        return (14 * depth) % 16, (14 * depth + 7) % 16

    unit = 2.0 * math.pi / (2 * HALF)

    def make_phase(depth, omega):
        speed = refs[depth, 0:1, 0:1] * omega
        speed2 = speed * speed
        forward_power, inverse_power = scale_power(depth)
        power = jnp.asarray(forward_power + inverse_power).astype(f32)
        gain = jnp.exp2(jnp.full((1, 1), 1.0, f32) * power * (-0.125))

        def phase_tile(row, col, row_odd, col_odd):
            gains = gain * jnp.where(row == 0, 0.5, 1.0) * jnp.where(col == 0, 0.5, 1.0)
            row = jnp.where(row == 0, HALF, row) if row_odd else row
            col = jnp.where(col == 0, HALF, col) if col_odd else col
            wave_x, wave_y = row.astype(f32) * unit, col.astype(f32) * unit
            squared = speed2 - wave_x * wave_x - wave_y * wave_y
            root = jnp.sqrt(jnp.abs(squared))
            waving = squared > 0.0
            inside = jnp.where(waving, squared, 0.0)
            damping = jnp.where(waving, 1.0, jnp.exp(-root)) * gains
            sine = jnp.where(waving, series(inside, SIN_PHASE) * root, 0.0)
            return damping * series(inside, COS_PHASE), damping * sine

        @pl.loop(0, HALF // 8)
        def _(i):
            rows = pl.ds(pl.multiple_of(i * 8, 8), 8)
            row = iota2((8, HALF), 0) + i * 8
            col = iota2((8, HALF), 1)
            even = phase_tile(row, col, False, False)
            odd = phase_tile(row[:, :128], col[:, :128], False, True)
            for k in range(2):
                for p in range(2):
                    phase[depth, 0, p, k, rows, :] = even[k]
                    phase[depth, 1, p, k, rows, 0:128] = odd[k]
                    phase[depth, 1, p, k, rows, 128:256] = even[k][:, 128:]

        row, col = iota2((8, HALF), 0), iota2((8, HALF), 1)
        for q in range(2):
            tile = phase_tile(row, col, True, q == 1)
            for k in range(2):
                phase[depth, q, 1, k, 0:8, :] = tile[k]

    @pl.when(chain_here)
    def _():
        for p in range(2):
            for dest, dims in ((base, (0, 1)), (base_t, (1, 0))):
                n = iota2((HALF, HALF), dims[0])
                k = iota2((HALF, HALF), dims[1])
                if p == 1:
                    k = jnp.where(k == 0, HALF, k)
                angle = ((2 * n + 1) * k % (4 * HALF)).astype(f32) * (2.0 * math.pi / (4 * HALF))
                dest[p] = (jnp.cos(angle) if p == 0 else jnp.sin(angle)) * 0.0625
            row, col = iota2((HALF, HALF), 0), iota2((HALF, HALF), 1)
            near = jnp.where(jnp.abs(row - col) == 1, 1.0, jnp.where(row == col, -2.0, 0.0))
            corner = jnp.logical_and(row == col, jnp.logical_or(row == 0, row == HALF - 1))
            ridge[p] = jnp.where(corner, -1.0 if p == 0 else -3.0, near).astype(bf16)

        first = jnp.where(me_c < 2, 0, NZ - 1)
        pltpu.make_async_copy(refs.at[first], refs.at[first], refs_sem).wait()
        make_phase(first, omega_ref[me_c % 2])

    @pl.when(helper_here)
    def _():
        pltpu.make_async_copy(refs, refs, refs_sem).wait()

    pl.semaphore_wait(barrier, greetings)

    @pl.when(jnp.logical_and(at_end, r == FIRST_ROW))
    def _():
        for w in range(2):
            send_first_slow(w).start()

    @pl.when(r == REF_ROW)
    def _():
        @pl.loop(0, 4)
        def _(c):
            send_slow(c).start()

    @pl.when(at_end)
    def _():
        for w in range(2):
            send_plane(first_chain + w).start()
        for w in range(2):
            send_plane(first_chain + w).wait_send()

    @pl.when(far_wanted)
    def _():
        send_far().start()

    @pl.when(early)
    def _():
        for w in range(2):
            @pl.when(direct(first_chain + w))
            def _():
                send_prep(first_chain + w).start()

    @pl.when(relay_here)
    def _():
        @pl.loop(0, relay_steps)
        def _(step):
            pass_depth(relay_depth(step))

    @pl.when(jnp.logical_or(chip_here, edge_here))
    def _():
        @pl.loop(0, 4)
        def _(c):
            @pl.when(jnp.logical_and(direct(c), jnp.logical_not(jnp.logical_and(chain_here, c == me_c))))
            def _():
                send_prep(c).start()

    @pl.when(jnp.logical_not(jnp.logical_or(chip_here, edge_here)))
    def _():
        start = jnp.where(d >= NZ // 2, 2, 0)

        @pl.loop(0, 4)
        def _(i):
            c = lax.rem(i + start, 4)
            asked = jnp.logical_and(d != 0, jnp.logical_not(jnp.logical_and(early, c // 2 == first_chain // 2)))

            @pl.when(jnp.logical_and(asked, direct(c)))
            def _():
                pl.semaphore_wait(ask_sem.at[c], 1)
                send_prep(c).start()

    def spread(step, row):
        source = me_c < 2
        target = jnp.where(source, step, NZ - 2 - step)
        to_side = row // 16
        block = jnp.where(to_side == 1, 31 - row, row)
        block = shipped.at[step, row % 4, to_side, block // 4]
        here = jnp.logical_and(target == d, row == r)

        @pl.when(here)
        def _():
            pltpu.make_async_copy(block, arrived.at[me_c], spread_sem.at[step]).start()

        @pl.when(jnp.logical_not(here))
        def _():
            pltpu.make_async_remote_copy(
                block, arrived.at[me_c], spread_sem.at[step], arrived_sem.at[me_c],
                device_id=(target, row), device_id_type=MESH,
            ).start()

    my_steps = jnp.where(me_c < 2, NZ, NZ - 1)

    def ask(step):
        depth = jnp.where(me_c < 2, step, NZ - 1 - step)

        @pl.when(step < my_steps)
        def _():
            @pl.loop(0, NROW)
            def _(i):
                @pl.when(jnp.logical_not(jnp.logical_or(unasked(depth, i), jnp.logical_and(i % 4 == (me_c + 2) % 4, i // 4 != 2 * me_c))))
                def _():
                    pl.semaphore_signal(ask_sem.at[me_c], inc=1, device_id=(depth, i), device_id_type=MESH)

    @pl.when(edge_here)
    def _():
        pl.semaphore_wait(ready_sem, 1)

        @pl.when(y == (me_c + 1) % 4)
        def _():
            ask(2)
            ask(3)
            ask(4)

        @pl.loop(0, my_steps)
        def _(step):
            pltpu.make_async_copy(shipped.at[step, 0], shipped.at[step, 0], landed_sem.at[step]).wait()

            @pl.when(y == (me_c + 1) % 4)
            def _():
                ask(step + 5)

            @pl.loop(0, 8)
            def _(i):
                spread(step, 4 * i + y)

        @pl.loop(0, my_steps)
        def _(step):
            pltpu.make_async_copy(shipped.at[step, 0], shipped.at[step, 0], spread_sem.at[step]).wait()

    def run_helper():
        source = me_c < 2
        omega = omega_ref[me_c % 2]
        steps = my_steps
        depth_of = relay_depth

        for other in (1, 3):
            pl.semaphore_signal(ready_sem, inc=1, device_id=(d, 8 * me_c + (me_c + other) % 4), device_id_type=MESH)

        def send_phase(depth):
            return pltpu.make_async_remote_copy(
                phase.at[depth], phase.at[depth], phase_out_sem.at[depth], phase_sem.at[depth],
                device_id=(d - 1, r), device_id_type=MESH,
            )

        def forward_rows(step):
            half = shipped.at[step, pl.ds(0, 2)]
            pltpu.make_async_copy(half, half, landed_sem.at[step]).wait()

            @pl.loop(0, 16)
            def _(i):
                spread(step, 4 * (i // 2) + (y + 2 * (i % 2)) % 4)

        make_phase(depth_of(1), omega)
        send_phase(depth_of(1)).start()

        @pl.loop(-2, steps)
        def _(step):
            @pl.when(step >= 0)
            def _():
                forward_rows(step)

            @pl.when(step + 4 < steps)
            def _():
                depth = depth_of(step + 4)
                make_phase(depth, omega)
                send_phase(depth).start()

        @pl.loop(0, steps)
        def _(step):
            @pl.when(step > 0)
            def _():
                send_phase(depth_of(step)).wait_send()

            half = shipped.at[step, pl.ds(0, 2)]
            pltpu.make_async_copy(half, half, spread_sem.at[step]).wait()

    def run_chain(source):
        w = me_c % 2
        omega = omega_ref[w]

        first_depth = 0 if source else NZ - 1

        def depth_of(step):
            return step if source else NZ - 1 - step

        slot_side, slot_rows = row_slot(r)
        own = pltpu.make_async_copy(prep, coef.at[d, slot_side, slot_rows], coef_sem.at[d])
        own.start()

        def make_tables(depth):
            forward_power, inverse_power = scale_power(depth)
            for way, power in enumerate((forward_power, inverse_power)):
                scale = jnp.exp2(jnp.full((1, 1), 1.0, f32) * power.astype(f32) * 0.0625)
                for p in range(2):
                    table[way, p] = (base[p] * scale).astype(bf16)
                    table_t[way, p] = (base_t[p] * scale).astype(bf16)

        def propagate(depth):
            @pl.when(depth != first_depth)
            def _():
                pltpu.make_async_copy(phase.at[depth], phase.at[depth], phase_sem.at[depth]).wait()

            for q in range(2):
                for p in range(2):
                    half = dot(xb[q, p].reshape(2 * HALF, HALF), table[0, q]).astype(bf16)
                    yb[q, p] = half.reshape(2, HALF, HALF)
            for p in range(2):
                for q in range(2):
                    real = dot(table_t[0, p], yb[q, p, 0])
                    imag = dot(table_t[0, p], yb[q, p, 1])
                    cos = phase[depth, q, p, 0]
                    sin = phase[depth, q, p, 1]
                    if source:
                        turned = (real * cos - imag * sin, real * sin + imag * cos)
                    else:
                        turned = (real * cos + imag * sin, imag * cos - real * sin)
                    for k in range(2):
                        yb[q, p, k] = turned[k].astype(bf16)
            for p in range(2):
                for q in range(2):
                    for k in range(2):
                        xb[q, p, k] = dot(table[1, p], yb[q, p, k]).astype(bf16)
            for q in range(2):
                for p in range(2):
                    eb[q, p] = dot(xb[q, p].reshape(2 * HALF, HALF), table_t[1, q]).reshape(2, HALF, HALF)

        def laplace(blocks, q, p, k):
            values = blocks[q, p, k]
            return dot(values, ridge[q]) + dot(ridge[p], values)

        def unfold(parts):
            mixed = [[parts[q][0] + parts[q][1], parts[q][0] - parts[q][1]] for q in range(2)]
            return [[mixed[0][a] + mixed[1][a] for a in range(2)], [mixed[0][a] - mixed[1][a] for a in range(2)]]

        def tiles(body):
            @pl.loop(0, HALF // ROWS)
            def _(i):
                rows = pl.ds(pl.multiple_of(i * ROWS, ROWS), ROWS)
                for j in range(2):
                    body(i, rows, pl.ds(j * 128, 128))

        powers = [omega]
        for _ in range(6):
            powers.append(powers[-1] * omega)
        cos_lens = [COS_LENS[0]] + [COS_LENS[k] * powers[2 * k - 1] for k in range(1, 4)]
        sin_lens = [SIN_LENS[k] * powers[2 * k] for k in range(4)]

        def lens_of(depth, b, a, i, cols):
            offset = coef[depth, a, i, 0, b, :, cols].astype(f32)
            square = offset * offset
            return series(square, cos_lens), series(square, sin_lens) * offset

        def ship_part(step, other):
            to_y = (y + other) % 4
            part = shipped.at[step, to_y]
            to_row = 4 * z + (to_y if other % 2 else y)
            return pltpu.make_async_remote_copy(
                part, part, ship_sem.at[step], landed_sem.at[step], device_id=(d + 1, to_row), device_id_type=MESH
            )

        def ship(step):
            for other in (1, 3, 0, 2):
                ship_part(step, other).start()

        def wait_coef(depth):
            pltpu.make_async_copy(coef.at[depth], coef.at[depth], coef_sem.at[depth]).wait()

        steps = NZ if source else NZ - 1
        pltpu.make_async_copy(plane, plane, plane_sem).wait()

        def first_fold(i, rows, cols):
            for k in range(2):
                folded = unfold([[plane[a, i, k, b, :, cols].astype(f32) for a in range(2)] for b in range(2)])
                for q in range(2):
                    for p in range(2):
                        if source:
                            xb[q, p, k, rows, cols] = folded[q][p].astype(bf16)
                        else:
                            eb[q, p, k, rows, cols] = folded[q][p] * 0.25
                            gb[q, p, k, rows, cols] = (folded[q][p] * 0.25).astype(bf16)

        tiles(first_fold)

        if source:
            @pl.loop(0, steps)
            def _(step):
                depth = depth_of(step)
                make_tables(depth)
                propagate(depth)
                wait_coef(depth)

                def spatial(i, rows, cols):
                    real = unfold([[eb[q, p, 0, rows, cols] for p in range(2)] for q in range(2)])
                    imag = unfold([[eb[q, p, 1, rows, cols] for p in range(2)] for q in range(2)])
                    lensed = [[[None, None], [None, None]] for _ in range(2)]
                    scaled = [[[None, None], [None, None]] for _ in range(2)]
                    for b in range(2):
                        for a in range(2):
                            cos, sin = lens_of(depth, b, a, i, cols)
                            factor = coef[depth, a, i, 1, b, :, cols].astype(f32)
                            lensed[0][b][a] = real[b][a] * cos - imag[b][a] * sin
                            lensed[1][b][a] = real[b][a] * sin + imag[b][a] * cos
                            for k in range(2):
                                scaled[k][b][a] = lensed[k][b][a] * factor
                    for k in range(2):
                        wave, bend = unfold(lensed[k]), unfold(scaled[k])
                        for q in range(2):
                            for p in range(2):
                                wb[q, p, k, rows, cols] = wave[q][p]
                                gb[q, p, k, rows, cols] = bend[q][p].astype(bf16)

                tiles(spatial)
                for q in range(2):
                    new = []
                    for p in range(2):
                        real = wb[q, p, 0] - laplace(gb, q, p, 1)
                        imag = wb[q, p, 1] + laplace(gb, q, p, 0)
                        xb[q, p, 0] = real.astype(bf16)
                        xb[q, p, 1] = imag.astype(bf16)
                        new.append((real * 0.25, imag * 0.25))
                    for k in range(2):
                        sides = ((new[0][k] + new[1][k]).astype(bf16), (new[0][k] - new[1][k]).astype(bf16))
                        for a, values in enumerate(sides):
                            values = values.reshape(4, 4, ROWS, HALF)
                            for i in range(4):
                                shipped[step, i if a == 0 else 3 - i, a, :, q, k] = values[:, i]
                ship(step)
        else:
            @pl.loop(0, steps)
            def _(step):
                depth = depth_of(step)
                make_tables(depth)
                for q in range(2):
                    for p in range(2):
                        for k in range(2):
                            wb[q, p, k] = laplace(gb, q, p, k)
                wait_coef(depth)

                def spatial(i, rows, cols):
                    value = [unfold([[eb[q, p, k, rows, cols] for p in range(2)] for q in range(2)]) for k in range(2)]
                    bend = [unfold([[wb[q, p, k, rows, cols] for p in range(2)] for q in range(2)]) for k in range(2)]
                    pulled = [[[None, None], [None, None]] for _ in range(2)]
                    for b in range(2):
                        for a in range(2):
                            cos, sin = lens_of(depth, b, a, i, cols)
                            factor = coef[depth, a, i, 1, b, :, cols].astype(f32)
                            real = value[0][b][a] + factor * bend[1][b][a]
                            imag = value[1][b][a] - factor * bend[0][b][a]
                            pulled[0][b][a] = real * cos + imag * sin
                            pulled[1][b][a] = imag * cos - real * sin
                    for k in range(2):
                        folded = unfold(pulled[k])
                        for q in range(2):
                            for p in range(2):
                                xb[q, p, k, rows, cols] = folded[q][p].astype(bf16)

                tiles(spatial)
                propagate(depth)

                def finish(i, rows, cols):
                    for q in range(2):
                        for k in range(2):
                            even, odd = eb[q, 0, k, rows, cols], eb[q, 1, k, rows, cols]
                            gb[q, 0, k, rows, cols] = even.astype(bf16)
                            gb[q, 1, k, rows, cols] = odd.astype(bf16)
                            shipped[step, i % 4, 0, i // 4, q, k, :, cols] = (even + odd).astype(bf16)
                            shipped[step, 3 - i % 4, 1, i // 4, q, k, :, cols] = (even - odd).astype(bf16)

                tiles(finish)
                ship(step)

        @pl.loop(0, steps)
        def _(step):
            pltpu.make_async_copy(shipped.at[step], shipped.at[step], ship_sem.at[step]).wait()

    @pl.when(helper_here)
    def _():
        run_helper()

    @pl.when(jnp.logical_and(chain_here, me_c < 2))
    def _():
        run_chain(True)

    @pl.when(jnp.logical_and(chain_here, me_c >= 2))
    def _():
        run_chain(False)

    def arrival(c):
        kept = jnp.logical_and(jnp.logical_or(helper_here, edge_here), me_c == c)

        @pl.when(jnp.logical_not(kept))
        def _():
            pltpu.make_async_copy(arrived.at[c], arrived.at[c], arrived_sem.at[c]).wait()

    for c in range(2):
        arrival(c)

    @pl.when(d != NZ - 1)
    def _():
        for c in range(2, 4):
            arrival(c)

    last = d == NZ - 1
    total = [None, None]
    for w in range(2):
        below = [[arrived[w, q, k].astype(f32) for k in range(2)] for q in range(2)]
        above = [[arrived[2 + w, q, k].astype(f32) for k in range(2)] for q in range(2)]
        for b in range(2):
            sign = 1.0 if b == 0 else -1.0
            down = [below[0][k] + sign * below[1][k] for k in range(2)]
            up = [
                jnp.where(last, prep_plane[w, k, b].astype(f32), above[0][k] + sign * above[1][k])
                for k in range(2)
            ]
            term = omega_ref[w] * (down[0] * up[1] - down[1] * up[0])
            total[b] = term if total[b] is None else total[b] + term
    exact = lax.Precision.HIGHEST
    total = [dot(turn, part, exact) for part in total]
    out_ref[:, :HALF] = total[0]
    out_ref[:, HALF:] = dot(total[1], exchange(HALF), exact)

    @pl.loop(0, 4)
    def _(c):
        sent = jnp.logical_and(jnp.logical_not(jnp.logical_and(chain_here, me_c == c)), jnp.logical_or(d != 0, c < 2))

        @pl.when(sent)
        def _():
            send_prep(c).wait_send()

        @pl.when(r == REF_ROW)
        def _():
            send_slow(c).wait_send()

    @pl.when(jnp.logical_and(at_end, r == FIRST_ROW))
    def _():
        for w in range(2):
            send_first_slow(w).wait_send()

    @pl.when(relay_here)
    def _():
        @pl.loop(0, relay_steps)
        def _(step):
            send_onward(relay_depth(step)).wait_send()


def per_device(source_top, adjoint_bottom, slowness, correction, slowness_ref, omega):
    vmem = pl.BlockSpec(memory_space=pltpu.VMEM)
    smem = pl.BlockSpec(memory_space=pltpu.SMEM)
    dma, plain = pltpu.SemaphoreType.DMA, pltpu.SemaphoreType.REGULAR
    block = (HALF, HALF)
    gradient = pl.pallas_call(
        kernel,
        out_shape=jax.ShapeDtypeStruct((ROWS, 2 * HALF), f32),
        in_specs=[vmem, vmem, vmem, vmem, smem, smem],
        out_specs=vmem,
        scratch_shapes=[
            pltpu.VMEM((2, 2, ROWS, HALF), bf16),
            pltpu.VMEM((2, 2, 2, ROWS, HALF), bf16),
            pltpu.VMEM((8, 128), f32),
            pltpu.VMEM((NZ, 2, 16, 2, 2, ROWS, HALF), bf16),
            pltpu.VMEM((2, 16, 2, 2, ROWS, HALF), bf16),
            pltpu.VMEM((NZ, 8, 128), f32),
            pltpu.VMEM((4, 2, 2, ROWS, HALF), bf16),
            pltpu.VMEM((NZ, 2, 2, 2) + block, f32),
            pltpu.VMEM((2,) + block, f32),
            pltpu.VMEM((2,) + block, f32),
            pltpu.VMEM((2, 2) + block, bf16),
            pltpu.VMEM((2, 2) + block, bf16),
            pltpu.VMEM((2,) + block, bf16),
            pltpu.VMEM((NZ, 4, 2, 4, 2, 2, ROWS, HALF), bf16),
            pltpu.VMEM((2, 2, 2) + block, bf16),
            pltpu.VMEM((2, 2, 2) + block, bf16),
            pltpu.VMEM((2, 2, 2) + block, bf16),
            pltpu.VMEM((2, 2, 2) + block, f32),
            pltpu.VMEM((2, 2, 2) + block, f32),
            dma((4,)),
            dma((2,)),
            dma((4,)),
            dma((NZ,)),
            dma(()),
            dma(()),
            dma((4,)),
            dma((NZ,)),
            plain((4,)),
            dma((NZ,)),
            dma((NZ,)),
            dma((NZ,)),
            dma((NZ,)),
            dma((2,)),
            plain(()),
            pltpu.VMEM((NZ, 2, 2, ROWS, HALF), bf16),
            dma((NZ,)),
            dma((NZ,)),
        ],
        compiler_params=pltpu.CompilerParams(
            collective_id=0, has_side_effects=True, vmem_limit_bytes=60 * 1024 * 1024
        ),
        name="imaging",
    )(slowness, correction, source_top, adjoint_bottom, slowness_ref, omega)
    return gradient[None]


def solution(mesh):
    in_specs = (
        P(None, None, "rows", None),
        P(None, None, "rows", None),
        P("depth", "rows", None),
        P("depth", "rows", None),
        P("depth"),
        P(),
    )
    return jax.shard_map(
        per_device, mesh=mesh, in_specs=in_specs, out_specs=P("depth", "rows", None), check_vma=False
    )
```

```python
import math

import jax
import jax.numpy as jnp
import numpy as np
from jax import lax
from jax.experimental import pallas as pl
from jax.experimental.pallas import tpu as pltpu
from jax.sharding import PartitionSpec as P

MESH = pl.DeviceIdType.MESH
f32, bf16 = jnp.float32, jnp.bfloat16
HALF = 256
ROWS = 16
NROW = 32
NZ = 8
REF_ROW = 5
FIRST_ROW = 6


def chain_depth(c):
    return 2 + 2 * (c % 2)


def chain_row(c):
    return 9 * c


def on_chain_chip(d, r):
    return jnp.logical_and(r % 9 == 0, d // 2 == 1 + (r // 9) % 2)


def on_edge(d, r):
    c = r // 8
    even = jnp.logical_and((r // 4) % 2 == 0, (r + c) % 2 == 1)
    return jnp.logical_and(even, d == 3 + 2 * (c % 2))


def unasked(d, r):
    return jnp.logical_or(on_chain_chip(d, r), on_edge(d, r))


def dot(a, b, precision=None):
    return jnp.dot(a, b, preferred_element_type=f32, precision=precision)


def iota2(shape, dim):
    return lax.broadcasted_iota(jnp.int32, shape, dim)


def exchange(size, flipped=True):
    row, col = iota2((size, size), 0), iota2((size, size), 1)
    target = jnp.where(flipped, size - 1 - row, row)
    return jnp.where(col == target, 1.0, 0.0).astype(f32)


def series(t, coefs):
    total = t * coefs[-1] + coefs[-2]
    for coef in coefs[-3::-1]:
        total = total * t + coef
    return total


LENS_REACH = 0.42


def fitted(function, reach):
    fit = np.polynomial.Chebyshev.interpolate(lambda t: function(np.sqrt(np.maximum(t, 1e-30))), 3, domain=(0.0, reach))
    return [float(coef) for coef in fit.convert(kind=np.polynomial.Polynomial).coef]


COS_LENS = fitted(np.cos, LENS_REACH)
SIN_LENS = fitted(lambda a: np.sin(a) / a, LENS_REACH)
COS_PHASE = [(-1.0) ** k / math.factorial(2 * k) for k in range(9)]
SIN_PHASE = [(-1.0) ** k / math.factorial(2 * k + 1) for k in range(8)]


def row_slot(r):
    side = r // 16
    block = jnp.where(side == 1, 31 - r, r)
    return side, block


def kernel(
    slow_ref, corr_ref, src_ref, adj_ref, ref_ref, omega_ref, out_ref,
    prep, prep_plane, prep_slow,
    coef, plane, refs, arrived,
    phase, base, base_t, table, table_t, ridge,
    shipped, xb, yb, gb, eb, wb,
    prep_sem, prep_plane_sem, prep_slow_sem,
    coef_sem, plane_sem, refs_sem, arrived_sem, ship_sem, ask_sem, landed_sem, spread_sem, phase_sem, phase_out_sem,
    first_slow_sem, ready_sem, relayed, relay_sem, onward_sem,
):
    d = lax.axis_index("depth")
    r = lax.axis_index("rows")
    side = r // 16
    barrier = pltpu.get_barrier_semaphore()
    z, y = r // 4, r % 4
    me_c = z // 2
    chip_here = on_chain_chip(d, r)
    chain_here = jnp.logical_and(chip_here, d % 2 == 0)
    helper_here = jnp.logical_and(chip_here, d % 2 == 1)
    edge_here = on_edge(d, r)
    relay_here = jnp.logical_and(d == 3 + 2 * (y % 2), z != 2 * y)
    at_end = jnp.logical_or(d == 0, d == NZ - 1)
    early = jnp.logical_or(d <= 1, d >= NZ - 2)
    first_chain = jnp.where(d <= 1, 0, 2)
    far_c = (y + 2) % 4
    far_here = z != 2 * far_c

    def direct(c):
        return jnp.logical_or(c != far_c, jnp.logical_not(far_here))

    def greet(depth, row):
        pl.semaphore_signal(barrier, inc=1, device_id=(depth, row), device_id_type=MESH)

    @pl.when(chain_here)
    def _():
        first = jnp.where(me_c < 2, 0, NZ - 1)

        second = jnp.where(me_c < 2, 1, NZ - 2)

        @pl.loop(0, NROW)
        def _(i):
            greet(first, i)

        @pl.loop(0, NROW)
        def _(i):
            greet(second, i)

        @pl.loop(0, 8)
        def _(i):
            @pl.when(i != z)
            def _():
                greet(d + 1, 4 * i + y)

        for c in range(4):
            @pl.when(c != me_c)
            def _():
                greet(chain_depth(c), chain_row(c))
            for other in (1, 3):
                greet(chain_depth(c) + 1, 8 * c + (c + other) % 4)

    @pl.when(jnp.logical_or(relay_here, helper_here))
    def _():
        @pl.loop(0, NZ)
        def _(i):
            greet(i, 4 * z + far_c)

    @pl.when(helper_here)
    def _():
        greet(d - 1, r)

        @pl.loop(0, NZ)
        def _(i):
            greet(i, REF_ROW)

    @pl.when(edge_here)
    def _():
        greet(d - 1, 9 * me_c)

    for c in range(4):
        @pl.when(jnp.logical_or(d != chain_depth(c) + 1, r != chain_row(c)))
        def _():
            greet(chain_depth(c) + 1, chain_row(c))

    turn = exchange(ROWS, side == 1)
    flip = exchange(HALF).astype(bf16)
    turn_b = turn.astype(bf16)

    def halves(values):
        turned = dot(turn_b, values).astype(bf16)
        return turned[:, :HALF], dot(turned[:, HALF:], flip).astype(bf16)

    slow_value = ref_ref[0]
    for k, values in enumerate((slow_ref[0] - slow_value, corr_ref[0])):
        left, right = halves(values.astype(bf16))
        prep[k, 0] = left
        prep[k, 1] = right
    prep_slow[...] = jnp.full((8, 128), slow_value, f32)

    def send_prep(c):
        slot_side, slot_rows = row_slot(r)
        return pltpu.make_async_remote_copy(
            prep, coef.at[d, slot_side, slot_rows], prep_sem.at[c], coef_sem.at[d],
            device_id=(chain_depth(c), chain_row(c)), device_id_type=MESH,
        )

    def send_plane(c):
        slot_side, slot_rows = row_slot(r)
        return pltpu.make_async_remote_copy(
            prep_plane.at[c % 2], plane.at[slot_side, slot_rows], prep_plane_sem.at[c % 2], plane_sem,
            device_id=(chain_depth(c), chain_row(c)), device_id_type=MESH,
        )

    def send_slow(c):
        return pltpu.make_async_remote_copy(
            prep_slow, refs.at[d], prep_slow_sem.at[c], refs_sem,
            device_id=(chain_depth(c) + 1, chain_row(c)), device_id_type=MESH,
        )

    far_device = (3 + 2 * (far_c % 2), 4 * z + far_c)
    far_wanted = jnp.logical_and(far_here, jnp.logical_or(d != 0, far_c < 2))

    def send_far():
        return pltpu.make_async_remote_copy(
            prep, relayed.at[d], prep_sem.at[far_c], relay_sem.at[d], device_id=far_device, device_id_type=MESH
        )

    def send_first_slow(w):
        return pltpu.make_async_remote_copy(
            prep_slow, refs.at[d], first_slow_sem.at[w], refs_sem,
            device_id=(chain_depth(first_chain + w), chain_row(first_chain + w)), device_id_type=MESH,
        )

    passed_side, passed_rows = row_slot(4 * z + far_c)
    passed_to = (chain_depth(y), chain_row(y))

    def send_onward(depth):
        return pltpu.make_async_remote_copy(
            relayed.at[depth], coef.at[depth, passed_side, passed_rows], onward_sem.at[depth], coef_sem.at[depth],
            device_id=passed_to, device_id_type=MESH,
        )

    def pass_depth(depth):
        pltpu.make_async_copy(relayed.at[depth], relayed.at[depth], relay_sem.at[depth]).wait()
        send_onward(depth).start()

    relay_steps = jnp.where(y < 2, NZ, NZ - 1)

    def relay_depth(step):
        return jnp.where(y < 2, step, NZ - 1 - step)

    @pl.when(d == 0)
    def _():
        for w in range(2):
            for k in range(2):
                left, right = halves(src_ref[w, k])
                prep_plane[w, k, 0] = left
                prep_plane[w, k, 1] = right

    @pl.when(d == NZ - 1)
    def _():
        for w in range(2):
            for k in range(2):
                left, right = halves(adj_ref[w, k])
                prep_plane[w, k, 0] = left
                prep_plane[w, k, 1] = right

    greetings = 1 + jnp.where(early, 2, 0) + jnp.where(r == REF_ROW, 4, 0)
    greetings = greetings + jnp.where(relay_here, 1, 0)
    greetings = greetings + jnp.where(edge_here, 4, 0)
    greetings = jnp.where(chain_here, 7, jnp.where(helper_here, 256, greetings))
    def scale_power(depth):
        return (14 * depth) % 16, (14 * depth + 7) % 16

    unit = 2.0 * math.pi / (2 * HALF)

    def make_phase(depth, omega):
        speed = refs[depth, 0:1, 0:1] * omega
        speed2 = speed * speed
        forward_power, inverse_power = scale_power(depth)
        power = jnp.asarray(forward_power + inverse_power).astype(f32)
        gain = jnp.exp2(jnp.full((1, 1), 1.0, f32) * power * (-0.125))

        def phase_tile(row, col, row_odd, col_odd):
            gains = gain * jnp.where(row == 0, 0.5, 1.0) * jnp.where(col == 0, 0.5, 1.0)
            row = jnp.where(row == 0, HALF, row) if row_odd else row
            col = jnp.where(col == 0, HALF, col) if col_odd else col
            wave_x, wave_y = row.astype(f32) * unit, col.astype(f32) * unit
            squared = speed2 - wave_x * wave_x - wave_y * wave_y
            root = jnp.sqrt(jnp.abs(squared))
            waving = squared > 0.0
            inside = jnp.where(waving, squared, 0.0)
            damping = jnp.where(waving, 1.0, jnp.exp(-root)) * gains
            sine = jnp.where(waving, series(inside, SIN_PHASE) * root, 0.0)
            return damping * series(inside, COS_PHASE), damping * sine

        @pl.loop(0, HALF // 8)
        def _(i):
            rows = pl.ds(pl.multiple_of(i * 8, 8), 8)
            row = iota2((8, HALF), 0) + i * 8
            col = iota2((8, HALF), 1)
            even = phase_tile(row, col, False, False)
            odd = phase_tile(row[:, :128], col[:, :128], False, True)
            for k in range(2):
                for p in range(2):
                    phase[depth, 0, p, k, rows, :] = even[k]
                    phase[depth, 1, p, k, rows, 0:128] = odd[k]
                    phase[depth, 1, p, k, rows, 128:256] = even[k][:, 128:]

        row, col = iota2((8, HALF), 0), iota2((8, HALF), 1)
        for q in range(2):
            tile = phase_tile(row, col, True, q == 1)
            for k in range(2):
                phase[depth, q, 1, k, 0:8, :] = tile[k]

    @pl.when(chain_here)
    def _():
        for p in range(2):
            for dest, dims in ((base, (0, 1)), (base_t, (1, 0))):
                n = iota2((HALF, HALF), dims[0])
                k = iota2((HALF, HALF), dims[1])
                if p == 1:
                    k = jnp.where(k == 0, HALF, k)
                angle = ((2 * n + 1) * k % (4 * HALF)).astype(f32) * (2.0 * math.pi / (4 * HALF))
                dest[p] = (jnp.cos(angle) if p == 0 else jnp.sin(angle)) * 0.0625
            row, col = iota2((HALF, HALF), 0), iota2((HALF, HALF), 1)
            near = jnp.where(jnp.abs(row - col) == 1, 1.0, jnp.where(row == col, -2.0, 0.0))
            corner = jnp.logical_and(row == col, jnp.logical_or(row == 0, row == HALF - 1))
            ridge[p] = jnp.where(corner, -1.0 if p == 0 else -3.0, near).astype(bf16)

        first = jnp.where(me_c < 2, 0, NZ - 1)
        pltpu.make_async_copy(refs.at[first], refs.at[first], refs_sem).wait()
        make_phase(first, omega_ref[me_c % 2])

    @pl.when(helper_here)
    def _():
        pltpu.make_async_copy(refs, refs, refs_sem).wait()

    pl.semaphore_wait(barrier, greetings)

    @pl.when(jnp.logical_and(at_end, r == FIRST_ROW))
    def _():
        for w in range(2):
            send_first_slow(w).start()

    @pl.when(r == REF_ROW)
    def _():
        @pl.loop(0, 4)
        def _(c):
            send_slow(c).start()

    @pl.when(at_end)
    def _():
        for w in range(2):
            send_plane(first_chain + w).start()
        for w in range(2):
            send_plane(first_chain + w).wait_send()

    @pl.when(far_wanted)
    def _():
        send_far().start()

    @pl.when(early)
    def _():
        for w in range(2):
            @pl.when(direct(first_chain + w))
            def _():
                send_prep(first_chain + w).start()

    @pl.when(relay_here)
    def _():
        @pl.loop(0, relay_steps)
        def _(step):
            pass_depth(relay_depth(step))

    @pl.when(jnp.logical_or(chip_here, edge_here))
    def _():
        @pl.loop(0, 4)
        def _(c):
            @pl.when(jnp.logical_and(direct(c), jnp.logical_not(jnp.logical_and(chain_here, c == me_c))))
            def _():
                send_prep(c).start()

    @pl.when(jnp.logical_not(jnp.logical_or(chip_here, edge_here)))
    def _():
        start = jnp.where(d >= NZ // 2, 2, 0)

        @pl.loop(0, 4)
        def _(i):
            c = lax.rem(i + start, 4)
            asked = jnp.logical_and(d != 0, jnp.logical_not(jnp.logical_and(early, c // 2 == first_chain // 2)))

            @pl.when(jnp.logical_and(asked, direct(c)))
            def _():
                pl.semaphore_wait(ask_sem.at[c], 1)
                send_prep(c).start()

    def spread(step, row):
        source = me_c < 2
        target = jnp.where(source, step, NZ - 2 - step)
        to_side = row // 16
        block = jnp.where(to_side == 1, 31 - row, row)
        block = shipped.at[step, row % 4, to_side, block // 4]
        here = jnp.logical_and(target == d, row == r)

        @pl.when(here)
        def _():
            pltpu.make_async_copy(block, arrived.at[me_c], spread_sem.at[step]).start()

        @pl.when(jnp.logical_not(here))
        def _():
            pltpu.make_async_remote_copy(
                block, arrived.at[me_c], spread_sem.at[step], arrived_sem.at[me_c],
                device_id=(target, row), device_id_type=MESH,
            ).start()

    my_steps = jnp.where(me_c < 2, NZ, NZ - 1)

    def ask(step):
        depth = jnp.where(me_c < 2, step, NZ - 1 - step)

        @pl.when(step < my_steps)
        def _():
            @pl.loop(0, NROW)
            def _(i):
                @pl.when(jnp.logical_not(jnp.logical_or(unasked(depth, i), jnp.logical_and(i % 4 == (me_c + 2) % 4, i // 4 != 2 * me_c))))
                def _():
                    pl.semaphore_signal(ask_sem.at[me_c], inc=1, device_id=(depth, i), device_id_type=MESH)

    @pl.when(edge_here)
    def _():
        pl.semaphore_wait(ready_sem, 1)

        @pl.when(y == (me_c + 1) % 4)
        def _():
            ask(2)
            ask(3)
            ask(4)

        @pl.loop(0, my_steps)
        def _(step):
            pltpu.make_async_copy(shipped.at[step, 0], shipped.at[step, 0], landed_sem.at[step]).wait()

            @pl.when(y == (me_c + 1) % 4)
            def _():
                ask(step + 5)

            @pl.loop(0, 8)
            def _(i):
                spread(step, 4 * i + y)

        @pl.loop(0, my_steps)
        def _(step):
            pltpu.make_async_copy(shipped.at[step, 0], shipped.at[step, 0], spread_sem.at[step]).wait()

    def run_helper():
        source = me_c < 2
        omega = omega_ref[me_c % 2]
        steps = my_steps
        depth_of = relay_depth

        for other in (1, 3):
            pl.semaphore_signal(ready_sem, inc=1, device_id=(d, 8 * me_c + (me_c + other) % 4), device_id_type=MESH)

        def send_phase(depth):
            return pltpu.make_async_remote_copy(
                phase.at[depth], phase.at[depth], phase_out_sem.at[depth], phase_sem.at[depth],
                device_id=(d - 1, r), device_id_type=MESH,
            )

        def forward_rows(step):
            half = shipped.at[step, pl.ds(0, 2)]
            pltpu.make_async_copy(half, half, landed_sem.at[step]).wait()

            @pl.loop(0, 16)
            def _(i):
                spread(step, 4 * (i // 2) + (y + 2 * (i % 2)) % 4)

        make_phase(depth_of(1), omega)
        send_phase(depth_of(1)).start()

        @pl.loop(-2, steps)
        def _(step):
            @pl.when(step >= 0)
            def _():
                forward_rows(step)

            @pl.when(step + 4 < steps)
            def _():
                depth = depth_of(step + 4)
                make_phase(depth, omega)
                send_phase(depth).start()

        @pl.loop(0, steps)
        def _(step):
            @pl.when(step > 0)
            def _():
                send_phase(depth_of(step)).wait_send()

            half = shipped.at[step, pl.ds(0, 2)]
            pltpu.make_async_copy(half, half, spread_sem.at[step]).wait()

    def run_chain(source):
        w = me_c % 2
        omega = omega_ref[w]

        first_depth = 0 if source else NZ - 1

        def depth_of(step):
            return step if source else NZ - 1 - step

        slot_side, slot_rows = row_slot(r)
        own = pltpu.make_async_copy(prep, coef.at[d, slot_side, slot_rows], coef_sem.at[d])
        own.start()

        def make_tables(depth):
            forward_power, inverse_power = scale_power(depth)
            for way, power in enumerate((forward_power, inverse_power)):
                scale = jnp.exp2(jnp.full((1, 1), 1.0, f32) * power.astype(f32) * 0.0625)
                for p in range(2):
                    table[way, p] = (base[p] * scale).astype(bf16)
                    table_t[way, p] = (base_t[p] * scale).astype(bf16)

        def pack(step, q, k, even, odd):
            for a, values in enumerate(((even + odd).astype(bf16), (even - odd).astype(bf16))):
                values = values.reshape(4, 4, ROWS, HALF)
                for i in range(4):
                    shipped[step, i if a == 0 else 3 - i, a, :, q, k] = values[:, i]

        def propagate(depth, step):
            @pl.when(depth != first_depth)
            def _():
                pltpu.make_async_copy(phase.at[depth], phase.at[depth], phase_sem.at[depth]).wait()

            for q in range(2):
                for p in range(2):
                    half = dot(xb[q, p].reshape(2 * HALF, HALF), table[0, q]).astype(bf16)
                    yb[q, p] = half.reshape(2, HALF, HALF)
            for p in range(2):
                for q in range(2):
                    real = dot(table_t[0, p], yb[q, p, 0])
                    imag = dot(table_t[0, p], yb[q, p, 1])
                    cos = phase[depth, q, p, 0]
                    sin = phase[depth, q, p, 1]
                    if source:
                        turned = (real * cos - imag * sin, real * sin + imag * cos)
                    else:
                        turned = (real * cos + imag * sin, imag * cos - real * sin)
                    for k in range(2):
                        yb[q, p, k] = turned[k].astype(bf16)
            for p in range(2):
                for q in range(2):
                    for k in range(2):
                        xb[q, p, k] = dot(table[1, p], yb[q, p, k]).astype(bf16)
            for q in range(2):
                parts = []
                for p in range(2):
                    part = dot(xb[q, p].reshape(2 * HALF, HALF), table_t[1, q]).reshape(2, HALF, HALF)
                    eb[q, p] = part
                    parts.append(part)
                if not source:
                    for p in range(2):
                        gb[q, p] = parts[p].astype(bf16)
                    for k in range(2):
                        pack(step, q, k, parts[0][k], parts[1][k])

        def laplace(blocks, q, p, k):
            values = blocks[q, p, k]
            return dot(values, ridge[q]) + dot(ridge[p], values)

        def unfold(parts):
            mixed = [[parts[q][0] + parts[q][1], parts[q][0] - parts[q][1]] for q in range(2)]
            return [[mixed[0][a] + mixed[1][a] for a in range(2)], [mixed[0][a] - mixed[1][a] for a in range(2)]]

        def tiles(body):
            @pl.loop(0, HALF // ROWS)
            def _(i):
                rows = pl.ds(pl.multiple_of(i * ROWS, ROWS), ROWS)
                for j in range(2):
                    body(i, rows, pl.ds(j * 128, 128))

        powers = [omega]
        for _ in range(6):
            powers.append(powers[-1] * omega)
        cos_lens = [COS_LENS[0]] + [COS_LENS[k] * powers[2 * k - 1] for k in range(1, 4)]
        sin_lens = [SIN_LENS[k] * powers[2 * k] for k in range(4)]

        def lens_of(depth, b, a, i, cols):
            offset = coef[depth, a, i, 0, b, :, cols].astype(f32)
            square = offset * offset
            return series(square, cos_lens), series(square, sin_lens) * offset

        def ship_part(step, other):
            to_y = (y + other) % 4
            part = shipped.at[step, to_y]
            to_row = 4 * z + (to_y if other % 2 else y)
            return pltpu.make_async_remote_copy(
                part, part, ship_sem.at[step], landed_sem.at[step], device_id=(d + 1, to_row), device_id_type=MESH
            )

        def ship(step):
            for other in (1, 3, 0, 2):
                ship_part(step, other).start()

        def wait_coef(depth):
            pltpu.make_async_copy(coef.at[depth], coef.at[depth], coef_sem.at[depth]).wait()

        steps = NZ if source else NZ - 1
        pltpu.make_async_copy(plane, plane, plane_sem).wait()

        def first_fold(i, rows, cols):
            for k in range(2):
                folded = unfold([[plane[a, i, k, b, :, cols].astype(f32) for a in range(2)] for b in range(2)])
                for q in range(2):
                    for p in range(2):
                        if source:
                            xb[q, p, k, rows, cols] = folded[q][p].astype(bf16)
                        else:
                            eb[q, p, k, rows, cols] = folded[q][p] * 0.25
                            gb[q, p, k, rows, cols] = (folded[q][p] * 0.25).astype(bf16)

        tiles(first_fold)

        if source:
            @pl.loop(0, steps)
            def _(step):
                depth = depth_of(step)
                make_tables(depth)
                propagate(depth, step)
                wait_coef(depth)

                def spatial(i, rows, cols):
                    real = unfold([[eb[q, p, 0, rows, cols] for p in range(2)] for q in range(2)])
                    imag = unfold([[eb[q, p, 1, rows, cols] for p in range(2)] for q in range(2)])
                    lensed = [[[None, None], [None, None]] for _ in range(2)]
                    scaled = [[[None, None], [None, None]] for _ in range(2)]
                    for b in range(2):
                        for a in range(2):
                            cos, sin = lens_of(depth, b, a, i, cols)
                            factor = coef[depth, a, i, 1, b, :, cols].astype(f32)
                            lensed[0][b][a] = real[b][a] * cos - imag[b][a] * sin
                            lensed[1][b][a] = real[b][a] * sin + imag[b][a] * cos
                            for k in range(2):
                                scaled[k][b][a] = lensed[k][b][a] * factor
                    for k in range(2):
                        wave, bend = unfold(lensed[k]), unfold(scaled[k])
                        for q in range(2):
                            for p in range(2):
                                wb[q, p, k, rows, cols] = wave[q][p]
                                gb[q, p, k, rows, cols] = bend[q][p].astype(bf16)

                tiles(spatial)
                for q in range(2):
                    new = []
                    for p in range(2):
                        real = wb[q, p, 0] - laplace(gb, q, p, 1)
                        imag = wb[q, p, 1] + laplace(gb, q, p, 0)
                        xb[q, p, 0] = real.astype(bf16)
                        xb[q, p, 1] = imag.astype(bf16)
                        new.append((real * 0.25, imag * 0.25))
                    for k in range(2):
                        pack(step, q, k, new[0][k], new[1][k])
                ship(step)
        else:
            @pl.loop(0, steps)
            def _(step):
                depth = depth_of(step)
                make_tables(depth)
                for q in range(2):
                    for p in range(2):
                        for k in range(2):
                            wb[q, p, k] = laplace(gb, q, p, k)
                wait_coef(depth)

                def spatial(i, rows, cols):
                    value = [unfold([[eb[q, p, k, rows, cols] for p in range(2)] for q in range(2)]) for k in range(2)]
                    bend = [unfold([[wb[q, p, k, rows, cols] for p in range(2)] for q in range(2)]) for k in range(2)]
                    pulled = [[[None, None], [None, None]] for _ in range(2)]
                    for b in range(2):
                        for a in range(2):
                            cos, sin = lens_of(depth, b, a, i, cols)
                            factor = coef[depth, a, i, 1, b, :, cols].astype(f32)
                            real = value[0][b][a] + factor * bend[1][b][a]
                            imag = value[1][b][a] - factor * bend[0][b][a]
                            pulled[0][b][a] = real * cos + imag * sin
                            pulled[1][b][a] = imag * cos - real * sin
                    for k in range(2):
                        folded = unfold(pulled[k])
                        for q in range(2):
                            for p in range(2):
                                xb[q, p, k, rows, cols] = folded[q][p].astype(bf16)

                tiles(spatial)
                propagate(depth, step)

                ship(step)

        @pl.loop(0, steps)
        def _(step):
            pltpu.make_async_copy(shipped.at[step], shipped.at[step], ship_sem.at[step]).wait()

    @pl.when(helper_here)
    def _():
        run_helper()

    @pl.when(jnp.logical_and(chain_here, me_c < 2))
    def _():
        run_chain(True)

    @pl.when(jnp.logical_and(chain_here, me_c >= 2))
    def _():
        run_chain(False)

    def arrival(c):
        kept = jnp.logical_and(jnp.logical_or(helper_here, edge_here), me_c == c)

        @pl.when(jnp.logical_not(kept))
        def _():
            pltpu.make_async_copy(arrived.at[c], arrived.at[c], arrived_sem.at[c]).wait()

    for c in range(2):
        arrival(c)

    @pl.when(d != NZ - 1)
    def _():
        for c in range(2, 4):
            arrival(c)

    last = d == NZ - 1
    total = [None, None]
    for w in range(2):
        below = [[arrived[w, q, k].astype(f32) for k in range(2)] for q in range(2)]
        above = [[arrived[2 + w, q, k].astype(f32) for k in range(2)] for q in range(2)]
        for b in range(2):
            sign = 1.0 if b == 0 else -1.0
            down = [below[0][k] + sign * below[1][k] for k in range(2)]
            up = [
                jnp.where(last, prep_plane[w, k, b].astype(f32), above[0][k] + sign * above[1][k])
                for k in range(2)
            ]
            term = omega_ref[w] * (down[0] * up[1] - down[1] * up[0])
            total[b] = term if total[b] is None else total[b] + term
    exact = lax.Precision.HIGHEST
    total = [dot(turn, part, exact) for part in total]
    out_ref[:, :HALF] = total[0]
    out_ref[:, HALF:] = dot(total[1], exchange(HALF), exact)

    @pl.loop(0, 4)
    def _(c):
        sent = jnp.logical_and(jnp.logical_not(jnp.logical_and(chain_here, me_c == c)), jnp.logical_or(d != 0, c < 2))

        @pl.when(sent)
        def _():
            send_prep(c).wait_send()

        @pl.when(r == REF_ROW)
        def _():
            send_slow(c).wait_send()

    @pl.when(jnp.logical_and(at_end, r == FIRST_ROW))
    def _():
        for w in range(2):
            send_first_slow(w).wait_send()

    @pl.when(relay_here)
    def _():
        @pl.loop(0, relay_steps)
        def _(step):
            send_onward(relay_depth(step)).wait_send()


def per_device(source_top, adjoint_bottom, slowness, correction, slowness_ref, omega):
    vmem = pl.BlockSpec(memory_space=pltpu.VMEM)
    smem = pl.BlockSpec(memory_space=pltpu.SMEM)
    dma, plain = pltpu.SemaphoreType.DMA, pltpu.SemaphoreType.REGULAR
    block = (HALF, HALF)
    gradient = pl.pallas_call(
        kernel,
        out_shape=jax.ShapeDtypeStruct((ROWS, 2 * HALF), f32),
        in_specs=[vmem, vmem, vmem, vmem, smem, smem],
        out_specs=vmem,
        scratch_shapes=[
            pltpu.VMEM((2, 2, ROWS, HALF), bf16),
            pltpu.VMEM((2, 2, 2, ROWS, HALF), bf16),
            pltpu.VMEM((8, 128), f32),
            pltpu.VMEM((NZ, 2, 16, 2, 2, ROWS, HALF), bf16),
            pltpu.VMEM((2, 16, 2, 2, ROWS, HALF), bf16),
            pltpu.VMEM((NZ, 8, 128), f32),
            pltpu.VMEM((4, 2, 2, ROWS, HALF), bf16),
            pltpu.VMEM((NZ, 2, 2, 2) + block, f32),
            pltpu.VMEM((2,) + block, f32),
            pltpu.VMEM((2,) + block, f32),
            pltpu.VMEM((2, 2) + block, bf16),
            pltpu.VMEM((2, 2) + block, bf16),
            pltpu.VMEM((2,) + block, bf16),
            pltpu.VMEM((NZ, 4, 2, 4, 2, 2, ROWS, HALF), bf16),
            pltpu.VMEM((2, 2, 2) + block, bf16),
            pltpu.VMEM((2, 2, 2) + block, bf16),
            pltpu.VMEM((2, 2, 2) + block, bf16),
            pltpu.VMEM((2, 2, 2) + block, f32),
            pltpu.VMEM((2, 2, 2) + block, f32),
            dma((4,)),
            dma((2,)),
            dma((4,)),
            dma((NZ,)),
            dma(()),
            dma(()),
            dma((4,)),
            dma((NZ,)),
            plain((4,)),
            dma((NZ,)),
            dma((NZ,)),
            dma((NZ,)),
            dma((NZ,)),
            dma((2,)),
            plain(()),
            pltpu.VMEM((NZ, 2, 2, ROWS, HALF), bf16),
            dma((NZ,)),
            dma((NZ,)),
        ],
        compiler_params=pltpu.CompilerParams(
            collective_id=0, has_side_effects=True, vmem_limit_bytes=60 * 1024 * 1024
        ),
        name="imaging",
    )(slowness, correction, source_top, adjoint_bottom, slowness_ref, omega)
    return gradient[None]


def solution(mesh):
    in_specs = (
        P(None, None, "rows", None),
        P(None, None, "rows", None),
        P("depth", "rows", None),
        P("depth", "rows", None),
        P("depth"),
        P(),
    )
    return jax.shard_map(
        per_device, mesh=mesh, in_specs=in_specs, out_specs=P("depth", "rows", None), check_vma=False
    )
```

```python
import math

import jax
import jax.numpy as jnp
import numpy as np
from jax import lax
from jax.experimental import pallas as pl
from jax.experimental.pallas import tpu as pltpu
from jax.sharding import PartitionSpec as P

MESH = pl.DeviceIdType.MESH
f32, bf16 = jnp.float32, jnp.bfloat16
HALF = 256
ROWS = 16
NROW = 32
NZ = 8
REF_ROW = 5
FIRST_ROW = 6


def chain_depth(c):
    return 2 + 2 * (c % 2)


def chain_row(c):
    return 9 * c


def on_chain_chip(d, r):
    return jnp.logical_and(r % 9 == 0, d // 2 == 1 + (r // 9) % 2)


def on_edge(d, r):
    c = r // 8
    even = jnp.logical_and((r // 4) % 2 == 0, (r + c) % 2 == 1)
    return jnp.logical_and(even, d == 3 + 2 * (c % 2))


def unasked(d, r):
    return jnp.logical_or(on_chain_chip(d, r), on_edge(d, r))


def dot(a, b, precision=None):
    return jnp.dot(a, b, preferred_element_type=f32, precision=precision)


def iota2(shape, dim):
    return lax.broadcasted_iota(jnp.int32, shape, dim)


def exchange(size, flipped=True):
    row, col = iota2((size, size), 0), iota2((size, size), 1)
    target = jnp.where(flipped, size - 1 - row, row)
    return jnp.where(col == target, 1.0, 0.0).astype(f32)


def series(t, coefs):
    total = t * coefs[-1] + coefs[-2]
    for coef in coefs[-3::-1]:
        total = total * t + coef
    return total


LENS_REACH = 0.42


def fitted(function, reach):
    fit = np.polynomial.Chebyshev.interpolate(lambda t: function(np.sqrt(np.maximum(t, 1e-30))), 3, domain=(0.0, reach))
    return [float(coef) for coef in fit.convert(kind=np.polynomial.Polynomial).coef]


COS_LENS = fitted(np.cos, LENS_REACH)
SIN_LENS = fitted(lambda a: np.sin(a) / a, LENS_REACH)
COS_PHASE = [(-1.0) ** k / math.factorial(2 * k) for k in range(9)]
SIN_PHASE = [(-1.0) ** k / math.factorial(2 * k + 1) for k in range(8)]


def row_slot(r):
    side = r // 16
    block = jnp.where(side == 1, 31 - r, r)
    return side, block


def kernel(
    slow_ref, corr_ref, src_ref, adj_ref, ref_ref, omega_ref, out_ref,
    prep, prep_plane, prep_slow,
    coef, plane, refs, arrived,
    phase, base, base_t, table, table_t, ridge,
    shipped, xb, yb, gb, eb, wb,
    prep_sem, prep_plane_sem, prep_slow_sem,
    coef_sem, plane_sem, refs_sem, arrived_sem, ship_sem, ask_sem, landed_sem, spread_sem, phase_sem, phase_out_sem,
    first_slow_sem, ready_sem, relayed, relay_sem, onward_sem,
):
    d = lax.axis_index("depth")
    r = lax.axis_index("rows")
    side = r // 16
    barrier = pltpu.get_barrier_semaphore()
    z, y = r // 4, r % 4
    me_c = z // 2
    chip_here = on_chain_chip(d, r)
    chain_here = jnp.logical_and(chip_here, d % 2 == 0)
    helper_here = jnp.logical_and(chip_here, d % 2 == 1)
    edge_here = on_edge(d, r)
    relay_here = jnp.logical_and(d == 3 + 2 * (y % 2), z != 2 * y)
    at_end = jnp.logical_or(d == 0, d == NZ - 1)
    early = jnp.logical_or(d <= 1, d >= NZ - 2)
    first_chain = jnp.where(d <= 1, 0, 2)
    far_c = (y + 2) % 4
    far_here = z != 2 * far_c

    def direct(c):
        return jnp.logical_or(c != far_c, jnp.logical_not(far_here))

    def greet(depth, row):
        pl.semaphore_signal(barrier, inc=1, device_id=(depth, row), device_id_type=MESH)

    @pl.when(chain_here)
    def _():
        first = jnp.where(me_c < 2, 0, NZ - 1)

        second = jnp.where(me_c < 2, 1, NZ - 2)

        @pl.loop(0, NROW)
        def _(i):
            greet(first, i)

        @pl.loop(0, NROW)
        def _(i):
            greet(second, i)

        @pl.loop(0, 8)
        def _(i):
            @pl.when(i != z)
            def _():
                greet(d + 1, 4 * i + y)

        for c in range(4):
            @pl.when(c != me_c)
            def _():
                greet(chain_depth(c), chain_row(c))
            for other in (1, 3):
                greet(chain_depth(c) + 1, 8 * c + (c + other) % 4)

    @pl.when(jnp.logical_or(relay_here, helper_here))
    def _():
        @pl.loop(0, NZ)
        def _(i):
            greet(i, 4 * z + far_c)

    @pl.when(helper_here)
    def _():
        greet(d - 1, r)

        @pl.loop(0, NZ)
        def _(i):
            greet(i, REF_ROW)

    @pl.when(edge_here)
    def _():
        greet(d - 1, 9 * me_c)

    for c in range(4):
        @pl.when(jnp.logical_or(d != chain_depth(c) + 1, r != chain_row(c)))
        def _():
            greet(chain_depth(c) + 1, chain_row(c))

    turn = exchange(ROWS, side == 1)
    flip = exchange(HALF).astype(bf16)
    turn_b = turn.astype(bf16)

    def halves(values):
        turned = dot(turn_b, values).astype(bf16)
        return turned[:, :HALF], dot(turned[:, HALF:], flip).astype(bf16)

    slow_value = ref_ref[0]
    for k, values in enumerate((slow_ref[0] - slow_value, corr_ref[0])):
        left, right = halves(values.astype(bf16))
        prep[k, 0] = left
        prep[k, 1] = right
    prep_slow[...] = jnp.full((8, 128), slow_value, f32)

    def send_prep(c):
        slot_side, slot_rows = row_slot(r)
        return pltpu.make_async_remote_copy(
            prep, coef.at[d, slot_side, slot_rows], prep_sem.at[c], coef_sem.at[d],
            device_id=(chain_depth(c), chain_row(c)), device_id_type=MESH,
        )

    def send_plane(c):
        slot_side, slot_rows = row_slot(r)
        return pltpu.make_async_remote_copy(
            prep_plane.at[c % 2], plane.at[slot_side, slot_rows], prep_plane_sem.at[c % 2], plane_sem,
            device_id=(chain_depth(c), chain_row(c)), device_id_type=MESH,
        )

    def send_slow(c):
        return pltpu.make_async_remote_copy(
            prep_slow, refs.at[d], prep_slow_sem.at[c], refs_sem,
            device_id=(chain_depth(c) + 1, chain_row(c)), device_id_type=MESH,
        )

    far_device = (3 + 2 * (far_c % 2), 4 * z + far_c)
    far_wanted = jnp.logical_and(far_here, jnp.logical_or(d != 0, far_c < 2))

    def send_far():
        return pltpu.make_async_remote_copy(
            prep, relayed.at[d], prep_sem.at[far_c], relay_sem.at[d], device_id=far_device, device_id_type=MESH
        )

    def send_first_slow(w):
        return pltpu.make_async_remote_copy(
            prep_slow, refs.at[d], first_slow_sem.at[w], refs_sem,
            device_id=(chain_depth(first_chain + w), chain_row(first_chain + w)), device_id_type=MESH,
        )

    passed_side, passed_rows = row_slot(4 * z + far_c)
    passed_to = (chain_depth(y), chain_row(y))

    def send_onward(depth):
        return pltpu.make_async_remote_copy(
            relayed.at[depth], coef.at[depth, passed_side, passed_rows], onward_sem.at[depth], coef_sem.at[depth],
            device_id=passed_to, device_id_type=MESH,
        )

    def pass_depth(depth):
        pltpu.make_async_copy(relayed.at[depth], relayed.at[depth], relay_sem.at[depth]).wait()
        send_onward(depth).start()

    relay_steps = jnp.where(y < 2, NZ, NZ - 1)

    def relay_depth(step):
        return jnp.where(y < 2, step, NZ - 1 - step)

    @pl.when(d == 0)
    def _():
        for w in range(2):
            for k in range(2):
                left, right = halves(src_ref[w, k])
                prep_plane[w, k, 0] = left
                prep_plane[w, k, 1] = right

    @pl.when(d == NZ - 1)
    def _():
        for w in range(2):
            for k in range(2):
                left, right = halves(adj_ref[w, k])
                prep_plane[w, k, 0] = left
                prep_plane[w, k, 1] = right

    greetings = 1 + jnp.where(early, 2, 0) + jnp.where(r == REF_ROW, 4, 0)
    greetings = greetings + jnp.where(relay_here, 1, 0)
    greetings = greetings + jnp.where(edge_here, 4, 0)
    greetings = jnp.where(chain_here, 7, jnp.where(helper_here, 256, greetings))
    def scale_power(depth):
        return (14 * depth) % 16, (14 * depth + 7) % 16

    unit = 2.0 * math.pi / (2 * HALF)

    def make_phase(depth, omega):
        speed = refs[depth, 0:1, 0:1] * omega
        speed2 = speed * speed
        forward_power, inverse_power = scale_power(depth)
        power = jnp.asarray(forward_power + inverse_power).astype(f32)
        gain = jnp.exp2(jnp.full((1, 1), 1.0, f32) * power * (-0.125))

        def phase_tile(row, col, row_odd, col_odd):
            gains = gain * jnp.where(row == 0, 0.5, 1.0) * jnp.where(col == 0, 0.5, 1.0)
            row = jnp.where(row == 0, HALF, row) if row_odd else row
            col = jnp.where(col == 0, HALF, col) if col_odd else col
            wave_x, wave_y = row.astype(f32) * unit, col.astype(f32) * unit
            squared = speed2 - wave_x * wave_x - wave_y * wave_y
            root = jnp.sqrt(jnp.abs(squared))
            waving = squared > 0.0
            inside = jnp.where(waving, squared, 0.0)
            damping = jnp.where(waving, 1.0, jnp.exp(-root)) * gains
            sine = jnp.where(waving, series(inside, SIN_PHASE) * root, 0.0)
            return damping * series(inside, COS_PHASE), damping * sine

        @pl.loop(0, HALF // 8)
        def _(i):
            rows = pl.ds(pl.multiple_of(i * 8, 8), 8)
            row = iota2((8, HALF), 0) + i * 8
            col = iota2((8, HALF), 1)
            even = phase_tile(row, col, False, False)
            odd = phase_tile(row[:, :128], col[:, :128], False, True)
            for k in range(2):
                for p in range(2):
                    phase[depth, 0, p, k, rows, :] = even[k]
                    phase[depth, 1, p, k, rows, 0:128] = odd[k]
                    phase[depth, 1, p, k, rows, 128:256] = even[k][:, 128:]

        row, col = iota2((8, HALF), 0), iota2((8, HALF), 1)
        for q in range(2):
            tile = phase_tile(row, col, True, q == 1)
            for k in range(2):
                phase[depth, q, 1, k, 0:8, :] = tile[k]

    @pl.when(chain_here)
    def _():
        for p in range(2):
            for dest, dims in ((base, (0, 1)), (base_t, (1, 0))):
                n = iota2((HALF, HALF), dims[0])
                k = iota2((HALF, HALF), dims[1])
                if p == 1:
                    k = jnp.where(k == 0, HALF, k)
                angle = ((2 * n + 1) * k % (4 * HALF)).astype(f32) * (2.0 * math.pi / (4 * HALF))
                dest[p] = (jnp.cos(angle) if p == 0 else jnp.sin(angle)) * 0.0625
            row, col = iota2((HALF, HALF), 0), iota2((HALF, HALF), 1)
            near = jnp.where(jnp.abs(row - col) == 1, 1.0, jnp.where(row == col, -2.0, 0.0))
            corner = jnp.logical_and(row == col, jnp.logical_or(row == 0, row == HALF - 1))
            ridge[p] = jnp.where(corner, -1.0 if p == 0 else -3.0, near).astype(bf16)

        first = jnp.where(me_c < 2, 0, NZ - 1)
        pltpu.make_async_copy(refs.at[first], refs.at[first], refs_sem).wait()
        make_phase(first, omega_ref[me_c % 2])

    @pl.when(helper_here)
    def _():
        pltpu.make_async_copy(refs, refs, refs_sem).wait()

    pl.semaphore_wait(barrier, greetings)

    @pl.when(jnp.logical_and(at_end, r == FIRST_ROW))
    def _():
        for w in range(2):
            send_first_slow(w).start()

    @pl.when(r == REF_ROW)
    def _():
        @pl.loop(0, 4)
        def _(c):
            send_slow(c).start()

    @pl.when(at_end)
    def _():
        for w in range(2):
            send_plane(first_chain + w).start()
        for w in range(2):
            send_plane(first_chain + w).wait_send()

    @pl.when(far_wanted)
    def _():
        send_far().start()

    @pl.when(early)
    def _():
        for w in range(2):
            @pl.when(direct(first_chain + w))
            def _():
                send_prep(first_chain + w).start()

    @pl.when(relay_here)
    def _():
        @pl.loop(0, relay_steps)
        def _(step):
            pass_depth(relay_depth(step))

    @pl.when(jnp.logical_or(chip_here, edge_here))
    def _():
        @pl.loop(0, 4)
        def _(c):
            @pl.when(jnp.logical_and(direct(c), jnp.logical_not(jnp.logical_and(chain_here, c == me_c))))
            def _():
                send_prep(c).start()

    @pl.when(jnp.logical_not(jnp.logical_or(chip_here, edge_here)))
    def _():
        start = jnp.where(d >= NZ // 2, 2, 0)

        @pl.loop(0, 4)
        def _(i):
            c = lax.rem(i + start, 4)
            asked = jnp.logical_and(d != 0, jnp.logical_not(jnp.logical_and(early, c // 2 == first_chain // 2)))

            @pl.when(jnp.logical_and(asked, direct(c)))
            def _():
                pl.semaphore_wait(ask_sem.at[c], 1)
                send_prep(c).start()

    def spread(step, row):
        source = me_c < 2
        target = jnp.where(source, step, NZ - 2 - step)
        to_side = row // 16
        block = jnp.where(to_side == 1, 31 - row, row)
        block = shipped.at[step, row % 4, to_side, block // 4]
        here = jnp.logical_and(target == d, row == r)

        @pl.when(here)
        def _():
            pltpu.make_async_copy(block, arrived.at[me_c], spread_sem.at[step]).start()

        @pl.when(jnp.logical_not(here))
        def _():
            pltpu.make_async_remote_copy(
                block, arrived.at[me_c], spread_sem.at[step], arrived_sem.at[me_c],
                device_id=(target, row), device_id_type=MESH,
            ).start()

    my_steps = jnp.where(me_c < 2, NZ, NZ - 1)

    def ask(step):
        depth = jnp.where(me_c < 2, step, NZ - 1 - step)

        @pl.when(step < my_steps)
        def _():
            @pl.loop(0, NROW)
            def _(i):
                @pl.when(jnp.logical_not(jnp.logical_or(unasked(depth, i), jnp.logical_and(i % 4 == (me_c + 2) % 4, i // 4 != 2 * me_c))))
                def _():
                    pl.semaphore_signal(ask_sem.at[me_c], inc=1, device_id=(depth, i), device_id_type=MESH)

    @pl.when(edge_here)
    def _():
        pl.semaphore_wait(ready_sem, 1)

        @pl.when(y == (me_c + 1) % 4)
        def _():
            ask(2)
            ask(3)
            ask(4)

        @pl.loop(0, my_steps)
        def _(step):
            pltpu.make_async_copy(shipped.at[step, 0], shipped.at[step, 0], landed_sem.at[step]).wait()

            @pl.when(y == (me_c + 1) % 4)
            def _():
                ask(step + 5)

            @pl.loop(0, 8)
            def _(i):
                spread(step, 4 * i + y)

        @pl.loop(0, my_steps)
        def _(step):
            pltpu.make_async_copy(shipped.at[step, 0], shipped.at[step, 0], spread_sem.at[step]).wait()

    def run_helper():
        source = me_c < 2
        omega = omega_ref[me_c % 2]
        steps = my_steps
        depth_of = relay_depth

        for other in (1, 3):
            pl.semaphore_signal(ready_sem, inc=1, device_id=(d, 8 * me_c + (me_c + other) % 4), device_id_type=MESH)

        def send_phase(depth):
            return pltpu.make_async_remote_copy(
                phase.at[depth], phase.at[depth], phase_out_sem.at[depth], phase_sem.at[depth],
                device_id=(d - 1, r), device_id_type=MESH,
            )

        def forward_rows(step):
            half = shipped.at[step, pl.ds(0, 2)]
            pltpu.make_async_copy(half, half, landed_sem.at[step]).wait()

            @pl.loop(0, 16)
            def _(i):
                spread(step, 4 * (i // 2) + (y + 2 * (i % 2)) % 4)

        make_phase(depth_of(1), omega)
        send_phase(depth_of(1)).start()

        @pl.loop(-2, steps)
        def _(step):
            @pl.when(step >= 0)
            def _():
                forward_rows(step)

            @pl.when(step + 4 < steps)
            def _():
                depth = depth_of(step + 4)
                make_phase(depth, omega)
                send_phase(depth).start()

        @pl.loop(0, steps)
        def _(step):
            @pl.when(step > 0)
            def _():
                send_phase(depth_of(step)).wait_send()

            half = shipped.at[step, pl.ds(0, 2)]
            pltpu.make_async_copy(half, half, spread_sem.at[step]).wait()

    def run_chain(source):
        w = me_c % 2
        omega = omega_ref[w]

        first_depth = 0 if source else NZ - 1

        def depth_of(step):
            return step if source else NZ - 1 - step

        slot_side, slot_rows = row_slot(r)
        own = pltpu.make_async_copy(prep, coef.at[d, slot_side, slot_rows], coef_sem.at[d])
        own.start()

        def make_tables(depth):
            forward_power, inverse_power = scale_power(depth)
            for way, power in enumerate((forward_power, inverse_power)):
                scale = jnp.exp2(jnp.full((1, 1), 1.0, f32) * power.astype(f32) * 0.0625)
                for p in range(2):
                    table[way, p] = (base[p] * scale).astype(bf16)
                    table_t[way, p] = (base_t[p] * scale).astype(bf16)

        def pack(step, q, k, even, odd):
            for a, values in enumerate(((even + odd).astype(bf16), (even - odd).astype(bf16))):
                values = values.reshape(4, 4, ROWS, HALF)
                for i in range(4):
                    shipped[step, i if a == 0 else 3 - i, a, :, q, k] = values[:, i]

        def propagate(depth, step):
            @pl.when(depth != first_depth)
            def _():
                pltpu.make_async_copy(phase.at[depth], phase.at[depth], phase_sem.at[depth]).wait()

            for q in range(2):
                for p in range(2):
                    half = dot(xb[q, p].reshape(2 * HALF, HALF), table[0, q]).astype(bf16)
                    yb[q, p] = half.reshape(2, HALF, HALF)
            for p in range(2):
                for q in range(2):
                    real = dot(table_t[0, p], yb[q, p, 0])
                    imag = dot(table_t[0, p], yb[q, p, 1])
                    cos = phase[depth, q, p, 0]
                    sin = phase[depth, q, p, 1]
                    if source:
                        turned = (real * cos - imag * sin, real * sin + imag * cos)
                    else:
                        turned = (real * cos + imag * sin, imag * cos - real * sin)
                    for k in range(2):
                        yb[q, p, k] = turned[k].astype(bf16)
            for p in range(2):
                for q in range(2):
                    for k in range(2):
                        xb[q, p, k] = dot(table[1, p], yb[q, p, k]).astype(bf16)
            for q in range(2):
                parts = []
                for p in range(2):
                    part = dot(xb[q, p].reshape(2 * HALF, HALF), table_t[1, q]).reshape(2, HALF, HALF)
                    eb[q, p] = part
                    parts.append(part)
                if not source:
                    for p in range(2):
                        gb[q, p] = parts[p].astype(bf16)
                    for k in range(2):
                        pack(step, q, k, parts[0][k], parts[1][k])

        def laplace(blocks, q, p, k):
            values = blocks[q, p, k]
            return dot(values, ridge[q]) + dot(ridge[p], values)

        def unfold(parts):
            mixed = [[parts[q][0] + parts[q][1], parts[q][0] - parts[q][1]] for q in range(2)]
            return [[mixed[0][a] + mixed[1][a] for a in range(2)], [mixed[0][a] - mixed[1][a] for a in range(2)]]

        def tiles(body):
            @pl.loop(0, HALF // ROWS, unroll=2)
            def _(i):
                rows = pl.ds(pl.multiple_of(i * ROWS, ROWS), ROWS)
                for j in range(2):
                    body(i, rows, pl.ds(j * 128, 128))

        powers = [omega]
        for _ in range(6):
            powers.append(powers[-1] * omega)
        cos_lens = [COS_LENS[0]] + [COS_LENS[k] * powers[2 * k - 1] for k in range(1, 4)]
        sin_lens = [SIN_LENS[k] * powers[2 * k] for k in range(4)]

        def lens_of(depth, b, a, i, cols):
            offset = coef[depth, a, i, 0, b, :, cols].astype(f32)
            square = offset * offset
            return series(square, cos_lens), series(square, sin_lens) * offset

        def ship_part(step, other):
            to_y = (y + other) % 4
            part = shipped.at[step, to_y]
            to_row = 4 * z + (to_y if other % 2 else y)
            return pltpu.make_async_remote_copy(
                part, part, ship_sem.at[step], landed_sem.at[step], device_id=(d + 1, to_row), device_id_type=MESH
            )

        def ship(step):
            for other in (1, 3, 0, 2):
                ship_part(step, other).start()

        def wait_coef(depth):
            pltpu.make_async_copy(coef.at[depth], coef.at[depth], coef_sem.at[depth]).wait()

        steps = NZ if source else NZ - 1
        pltpu.make_async_copy(plane, plane, plane_sem).wait()

        def first_fold(i, rows, cols):
            for k in range(2):
                folded = unfold([[plane[a, i, k, b, :, cols].astype(f32) for a in range(2)] for b in range(2)])
                for q in range(2):
                    for p in range(2):
                        if source:
                            xb[q, p, k, rows, cols] = folded[q][p].astype(bf16)
                        else:
                            eb[q, p, k, rows, cols] = folded[q][p] * 0.25
                            gb[q, p, k, rows, cols] = (folded[q][p] * 0.25).astype(bf16)

        tiles(first_fold)

        if source:
            @pl.loop(0, steps)
            def _(step):
                depth = depth_of(step)
                make_tables(depth)
                propagate(depth, step)
                wait_coef(depth)

                def spatial(i, rows, cols):
                    real = unfold([[eb[q, p, 0, rows, cols] for p in range(2)] for q in range(2)])
                    imag = unfold([[eb[q, p, 1, rows, cols] for p in range(2)] for q in range(2)])
                    lensed = [[[None, None], [None, None]] for _ in range(2)]
                    scaled = [[[None, None], [None, None]] for _ in range(2)]
                    for b in range(2):
                        for a in range(2):
                            cos, sin = lens_of(depth, b, a, i, cols)
                            factor = coef[depth, a, i, 1, b, :, cols].astype(f32)
                            lensed[0][b][a] = real[b][a] * cos - imag[b][a] * sin
                            lensed[1][b][a] = real[b][a] * sin + imag[b][a] * cos
                            for k in range(2):
                                scaled[k][b][a] = lensed[k][b][a] * factor
                    for k in range(2):
                        wave, bend = unfold(lensed[k]), unfold(scaled[k])
                        for q in range(2):
                            for p in range(2):
                                wb[q, p, k, rows, cols] = wave[q][p]
                                gb[q, p, k, rows, cols] = bend[q][p].astype(bf16)

                tiles(spatial)
                for q in range(2):
                    new = []
                    for p in range(2):
                        real = wb[q, p, 0] - laplace(gb, q, p, 1)
                        imag = wb[q, p, 1] + laplace(gb, q, p, 0)
                        xb[q, p, 0] = real.astype(bf16)
                        xb[q, p, 1] = imag.astype(bf16)
                        new.append((real * 0.25, imag * 0.25))
                    for k in range(2):
                        pack(step, q, k, new[0][k], new[1][k])
                ship(step)
        else:
            @pl.loop(0, steps)
            def _(step):
                depth = depth_of(step)
                make_tables(depth)
                for q in range(2):
                    for p in range(2):
                        for k in range(2):
                            wb[q, p, k] = laplace(gb, q, p, k)
                wait_coef(depth)

                def spatial(i, rows, cols):
                    value = [unfold([[eb[q, p, k, rows, cols] for p in range(2)] for q in range(2)]) for k in range(2)]
                    bend = [unfold([[wb[q, p, k, rows, cols] for p in range(2)] for q in range(2)]) for k in range(2)]
                    pulled = [[[None, None], [None, None]] for _ in range(2)]
                    for b in range(2):
                        for a in range(2):
                            cos, sin = lens_of(depth, b, a, i, cols)
                            factor = coef[depth, a, i, 1, b, :, cols].astype(f32)
                            real = value[0][b][a] + factor * bend[1][b][a]
                            imag = value[1][b][a] - factor * bend[0][b][a]
                            pulled[0][b][a] = real * cos + imag * sin
                            pulled[1][b][a] = imag * cos - real * sin
                    for k in range(2):
                        folded = unfold(pulled[k])
                        for q in range(2):
                            for p in range(2):
                                xb[q, p, k, rows, cols] = folded[q][p].astype(bf16)

                tiles(spatial)
                propagate(depth, step)

                ship(step)

        @pl.loop(0, steps)
        def _(step):
            pltpu.make_async_copy(shipped.at[step], shipped.at[step], ship_sem.at[step]).wait()

    @pl.when(helper_here)
    def _():
        run_helper()

    @pl.when(jnp.logical_and(chain_here, me_c < 2))
    def _():
        run_chain(True)

    @pl.when(jnp.logical_and(chain_here, me_c >= 2))
    def _():
        run_chain(False)

    def arrival(c):
        kept = jnp.logical_and(jnp.logical_or(helper_here, edge_here), me_c == c)

        @pl.when(jnp.logical_not(kept))
        def _():
            pltpu.make_async_copy(arrived.at[c], arrived.at[c], arrived_sem.at[c]).wait()

    for c in range(2):
        arrival(c)

    @pl.when(d != NZ - 1)
    def _():
        for c in range(2, 4):
            arrival(c)

    last = d == NZ - 1
    total = [None, None]
    for w in range(2):
        below = [[arrived[w, q, k].astype(f32) for k in range(2)] for q in range(2)]
        above = [[arrived[2 + w, q, k].astype(f32) for k in range(2)] for q in range(2)]
        for b in range(2):
            sign = 1.0 if b == 0 else -1.0
            down = [below[0][k] + sign * below[1][k] for k in range(2)]
            up = [
                jnp.where(last, prep_plane[w, k, b].astype(f32), above[0][k] + sign * above[1][k])
                for k in range(2)
            ]
            term = omega_ref[w] * (down[0] * up[1] - down[1] * up[0])
            total[b] = term if total[b] is None else total[b] + term
    exact = lax.Precision.HIGHEST
    total = [dot(turn, part, exact) for part in total]
    out_ref[:, :HALF] = total[0]
    out_ref[:, HALF:] = dot(total[1], exchange(HALF), exact)

    @pl.loop(0, 4)
    def _(c):
        sent = jnp.logical_and(jnp.logical_not(jnp.logical_and(chain_here, me_c == c)), jnp.logical_or(d != 0, c < 2))

        @pl.when(sent)
        def _():
            send_prep(c).wait_send()

        @pl.when(r == REF_ROW)
        def _():
            send_slow(c).wait_send()

    @pl.when(jnp.logical_and(at_end, r == FIRST_ROW))
    def _():
        for w in range(2):
            send_first_slow(w).wait_send()

    @pl.when(relay_here)
    def _():
        @pl.loop(0, relay_steps)
        def _(step):
            send_onward(relay_depth(step)).wait_send()


def per_device(source_top, adjoint_bottom, slowness, correction, slowness_ref, omega):
    vmem = pl.BlockSpec(memory_space=pltpu.VMEM)
    smem = pl.BlockSpec(memory_space=pltpu.SMEM)
    dma, plain = pltpu.SemaphoreType.DMA, pltpu.SemaphoreType.REGULAR
    block = (HALF, HALF)
    gradient = pl.pallas_call(
        kernel,
        out_shape=jax.ShapeDtypeStruct((ROWS, 2 * HALF), f32),
        in_specs=[vmem, vmem, vmem, vmem, smem, smem],
        out_specs=vmem,
        scratch_shapes=[
            pltpu.VMEM((2, 2, ROWS, HALF), bf16),
            pltpu.VMEM((2, 2, 2, ROWS, HALF), bf16),
            pltpu.VMEM((8, 128), f32),
            pltpu.VMEM((NZ, 2, 16, 2, 2, ROWS, HALF), bf16),
            pltpu.VMEM((2, 16, 2, 2, ROWS, HALF), bf16),
            pltpu.VMEM((NZ, 8, 128), f32),
            pltpu.VMEM((4, 2, 2, ROWS, HALF), bf16),
            pltpu.VMEM((NZ, 2, 2, 2) + block, f32),
            pltpu.VMEM((2,) + block, f32),
            pltpu.VMEM((2,) + block, f32),
            pltpu.VMEM((2, 2) + block, bf16),
            pltpu.VMEM((2, 2) + block, bf16),
            pltpu.VMEM((2,) + block, bf16),
            pltpu.VMEM((NZ, 4, 2, 4, 2, 2, ROWS, HALF), bf16),
            pltpu.VMEM((2, 2, 2) + block, bf16),
            pltpu.VMEM((2, 2, 2) + block, bf16),
            pltpu.VMEM((2, 2, 2) + block, bf16),
            pltpu.VMEM((2, 2, 2) + block, f32),
            pltpu.VMEM((2, 2, 2) + block, f32),
            dma((4,)),
            dma((2,)),
            dma((4,)),
            dma((NZ,)),
            dma(()),
            dma(()),
            dma((4,)),
            dma((NZ,)),
            plain((4,)),
            dma((NZ,)),
            dma((NZ,)),
            dma((NZ,)),
            dma((NZ,)),
            dma((2,)),
            plain(()),
            pltpu.VMEM((NZ, 2, 2, ROWS, HALF), bf16),
            dma((NZ,)),
            dma((NZ,)),
        ],
        compiler_params=pltpu.CompilerParams(
            collective_id=0, has_side_effects=True, vmem_limit_bytes=60 * 1024 * 1024
        ),
        name="imaging",
    )(slowness, correction, source_top, adjoint_bottom, slowness_ref, omega)
    return gradient[None]


def solution(mesh):
    in_specs = (
        P(None, None, "rows", None),
        P(None, None, "rows", None),
        P("depth", "rows", None),
        P("depth", "rows", None),
        P("depth"),
        P(),
    )
    return jax.shard_map(
        per_device, mesh=mesh, in_specs=in_specs, out_specs=P("depth", "rows", None), check_vma=False
    )
```
